128 devices in a mesh: req: 64 (over y, x, z), head: 2 (over core).
Axes of the slice: x: 4, y: 4, z: 4, core: 2. Of those that a mesh axis runs over, the one named last changes fastest.
Arguments:
- hidden_in: bfloat16 [4096, 2048], P('req'), may hold values from -14 to 14
- attn_gain: float32 [2048], replicated, may hold values from 0.1 to 1.9
- w_query: bfloat16 [2048, 2048], P(None, 'head'), may hold values from -0.125 to 0.125
- w_key: bfloat16 [2048, 1024], P(None, 'head'), may hold values from -0.125 to 0.125
- w_value: bfloat16 [2048, 1024], P(None, 'head'), may hold values from -0.125 to 0.125
- query_gain: float32 [128], replicated, may hold values from 0.5 to 2
- key_gain: float32 [128], replicated, may hold values from 0.5 to 2
- w_out: bfloat16 [2048, 2048], P('head'), may hold values from -0.125 to 0.125
- cache_keys: bfloat16 [64, 2048, 1024], P('req', None, 'head'), may hold values from -3.5 to 3.5
- cache_values: bfloat16 [64, 2048, 1024], P('req', None, 'head'), may hold values from -6 to 6
- cache_lengths: int32 [64], replicated, may hold values from 1 to 2048, 65536 in all
- slot_request: int32 [64], replicated, may hold values from 0 to 63, each once
- mlp_gain: float32 [2048], P('head'), may hold values from 0.1 to 1.9
- w_gate: bfloat16 [2048, 6144], P('head', 'req'), may hold values from -0.125 to 0.125
- w_up: bfloat16 [2048, 6144], P('head', 'req'), may hold values from -0.125 to 0.125
- w_down: bfloat16 [6144, 2048], P('req', 'head'), may hold values from -0.078125 to 0.078125
- final_gain: float32 [2048], replicated, may hold values from 0.1 to 1.9
- w_vocab: bfloat16 [2048, 151936], P(None, ('req', 'head')), may hold values from -8 to 8
Outputs:
- hidden_out: bfloat16 [4096, 2048], P('req', 'head')
- log_probs: float32 [64, 151936], P(None, ('req', 'head'))
The draws below stay inside these ranges and needn't reach their ends.
Inputs may be any that keep to these rules, and one draw needn't show every extreme that they name: `cache_lengths`: the largest length is exactly 2048. `slot_request`: each request appears once.
All inputs are finite; a program needn't handle non-finite values.
Results may differ from the reference program's by a relative error of at most 0.008.
Values may be sent and summed in bfloat16 or wider, within the bound.
A program may use at most 128 MiB of HBM per device.

```python
import math
import jax
import jax.numpy as jnp
import numpy as np
from jax import lax

D = 2048
HEADS_Q = 16
HEADS_KV = 8
HEAD_DIM = 128
FF = 6144
VOCAB = 151936
S_NEW = 64
LMAX = 2048
REQS = 64


def draw_w_vocab(key, part):
    normal_key, scale_key = jax.random.split(key)
    entries = jax.random.truncated_normal(normal_key, -4.0, 4.0, (D, VOCAB), jnp.float32)
    spread = jax.random.uniform(scale_key, (1, VOCAB), jnp.float32, 0.0, math.log(10.0))
    return jnp.clip(entries * jnp.exp(spread) * D ** (-0.5), -8.0, 8.0).astype(jnp.bfloat16)


def draw_hidden_in(key, part):
    entry_key = jax.random.fold_in(key, 17)
    columns = jnp.arange(D, dtype=jnp.float32) / (D - 1)
    entries = jax.random.truncated_normal(entry_key, -4.0, 4.0, (REQS * S_NEW, D), jnp.float32)
    column_scale = jnp.exp(math.log(3.5) * columns)
    return jnp.clip(entries * column_scale[None, :], -14.0, 14.0).astype(jnp.bfloat16)


def shard_levels(key, dims, cuts, least, largest):
    level, own = 1.0, jax.random.fold_in(key, 6)
    for axis_at, shards_of in cuts:
        draws = jnp.exp(jax.random.uniform(jax.random.fold_in(own, axis_at), (shards_of,), jnp.float32, least / len(cuts), largest / len(cuts)))
        level = level * jnp.repeat(draws, dims[axis_at] // shards_of).reshape([-1 if axis == axis_at else 1 for axis in range(len(dims))])
    return level


def split_up(count, total, bound, slope):
    weights = [(1 << 20) // math.isqrt(grade ** slope) + 1 for grade in range(2, count + 1)]
    spare, holding = total - bound - (count - 1), [1] * (count - 1)
    while spare > 0:
        free = [i for i in range(count - 1) if holding[i] < bound]
        pool, remaining = sum([weights[i] for i in free]), spare
        for i in free:
            extra = min(bound - holding[i], max(1, remaining * weights[i] // pool), spare)
            holding[i] = holding[i] + extra
            spare = spare - extra
    return np.array([bound] + holding)


def ragged(rng, amount, total, reach, skew):
    if amount == 2:
        one = jax.random.randint(rng, (), max(1, total - reach), min(reach, total - 1) + 1)
        return jnp.stack([one, total - one])
    sizes = jnp.asarray(split_up(amount, total, reach, skew), jnp.int32)
    twos = (amount - 1) // 2
    donor, sink = sizes[1:1 + 2 * twos:2], sizes[2:2 + 2 * twos:2]
    slack = jnp.minimum(donor - 1, reach - sink)
    shifted = jax.random.randint(jax.random.fold_in(rng, 1), (twos,), 0, 1 << 20) % (slack + 1)
    sizes = sizes.at[1:1 + 2 * twos:2].set(donor - shifted).at[2:2 + 2 * twos:2].set(sink + shifted)
    return sizes[jax.random.permutation(jax.random.fold_in(rng, 2), amount)]


def noise(rng, dims, deviation, reach, cuts=(), kind=jnp.bfloat16):
    array = jax.random.normal(rng, dims, jnp.float32) * deviation
    if len(cuts) > 0:
        array = shard_levels(rng, dims, cuts, -0.22, 0.18) * array
    return jnp.clip(array, min=-reach, max=reach).astype(kind)


def setup_inputs(seed: int = 0) -> dict:
    arg_keys = jax.random.split(jax.random.key(seed), 19)
    return {
        "hidden_in": draw_hidden_in(jax.random.fold_in(arg_keys[18], 71), 0),
        "attn_gain": jnp.clip(1.0 + 0.18 * jax.random.normal(arg_keys[1], (D,), jnp.float32), 0.1, 1.9),
        "w_query": noise(arg_keys[2], (D, HEADS_Q * HEAD_DIM), D ** -0.5, 0.125, ((1, 2),)),
        "w_key": noise(arg_keys[3], (D, HEADS_KV * HEAD_DIM), D ** -0.5, 0.125, ((1, 2),)),
        "w_value": noise(arg_keys[4], (D, HEADS_KV * HEAD_DIM), D ** -0.5, 0.125, ((1, 2),)),
        "query_gain": jnp.clip(jnp.exp(jax.random.uniform(arg_keys[5], (HEAD_DIM,), jnp.float32, math.log(0.5), math.log(2.0))), 0.5, 2.0),
        "key_gain": jnp.clip(jnp.exp(jax.random.uniform(arg_keys[6], (HEAD_DIM,), jnp.float32, math.log(0.5), math.log(2.0))), 0.5, 2.0),
        "w_out": noise(arg_keys[7], (HEADS_Q * HEAD_DIM, D), (HEADS_Q * HEAD_DIM) ** -0.5, 0.125, ((0, 2),)),
        "cache_keys": noise(arg_keys[8], (REQS, LMAX, HEADS_KV * HEAD_DIM), 1.0, 3.5, ((0, 64), (2, 2))),
        "cache_values": noise(arg_keys[9], (REQS, LMAX, HEADS_KV * HEAD_DIM), 1.0, 6.0, ((0, 64), (2, 2))),
        "cache_lengths": ragged(arg_keys[10], REQS, REQS * LMAX // 2, LMAX, 2).astype(jnp.int32),
        "slot_request": jax.random.permutation(arg_keys[11], REQS).astype(jnp.int32),
        "mlp_gain": jnp.clip(1.0 + 0.18 * jax.random.normal(arg_keys[12], (D,), jnp.float32), 0.1, 1.9),
        "w_gate": noise(arg_keys[13], (D, FF), D ** -0.5, 0.125, ((0, 2), (1, 64))),
        "w_up": noise(arg_keys[14], (D, FF), D ** -0.5, 0.125, ((0, 2), (1, 64))),
        "w_down": noise(arg_keys[15], (FF, D), FF ** -0.5, 0.078125, ((0, 64), (1, 2))),
        "final_gain": jnp.clip(1.0 + 0.18 * jax.random.normal(arg_keys[16], (D,), jnp.float32), 0.1, 1.9),
        "w_vocab": draw_w_vocab(jax.random.fold_in(arg_keys[18], 71), 0),
    }


EPS = 1e-06
ROPE_BASE = 1000000.0
NEG = -1e+30

def norm_rows(field, gain_vec):
    return field * lax.rsqrt(lax.optimization_barrier(jnp.mean(field * field, axis=-1, keepdims=True)) + EPS) * gain_vec

def rotate(field, positions):
    half_dim = field.shape[-1] // 2
    frequency = ROPE_BASE ** (-2.0 * jnp.arange(half_dim, dtype=jnp.float32) / field.shape[-1])
    angles = positions[..., None, None] * frequency
    cosine = jnp.cos(angles)
    sines = jnp.sin(angles)
    lower_half = field[..., :half_dim]
    upper_half = field[..., half_dim:]
    return jnp.concatenate([lower_half * cosine - upper_half * sines, upper_half * cosine + lower_half * sines], axis=-1)

def inverse_order(slot_request):
    indices = jnp.arange(slot_request.shape[0], dtype=jnp.int32)
    return lax.optimization_barrier(jnp.sum(jnp.where(slot_request[None, :] == indices[:, None], indices[None, :], 0), axis=1)).astype(jnp.int32)

def slot_attention(inputs):
    queries, keys_new, values_new, keys_cache, values_cache, cache_len = inputs
    group_size = HEADS_Q // HEADS_KV
    grouped = queries.astype(jnp.float32).reshape(S_NEW, HEADS_KV, group_size, HEAD_DIM)
    stored_keys = keys_cache.astype(jnp.float32).reshape(LMAX, HEADS_KV, HEAD_DIM)
    stored_values = values_cache.astype(jnp.float32).reshape(LMAX, HEADS_KV, HEAD_DIM)
    score_scale = HEAD_DIM ** (-0.5)
    stored = jnp.einsum('skgd,lkd->kgsl', grouped, stored_keys) * score_scale
    stored = jnp.where(jnp.arange(LMAX, dtype=jnp.int32) < cache_len, stored, NEG)
    recent = jnp.einsum('skgd,tkd->kgst', grouped, keys_new.astype(jnp.float32)) * score_scale
    causal = jnp.arange(S_NEW)[:, None] >= jnp.arange(S_NEW)[None, :]
    recent = jnp.where(causal, recent, NEG)
    old_weights = jnp.exp(stored)
    new_weights = jnp.exp(recent)
    row_total = lax.optimization_barrier(jnp.sum(old_weights, axis=-1)) + lax.optimization_barrier(jnp.sum(new_weights, axis=-1))
    old_weights = (old_weights / row_total[..., None]).astype(jnp.bfloat16)
    new_weights = (new_weights / row_total[..., None]).astype(jnp.bfloat16)
    blended = jnp.einsum('kgsl,lkd->skgd', old_weights.astype(jnp.float32), stored_values)
    blended = blended + jnp.einsum('kgst,tkd->skgd', new_weights.astype(jnp.float32), values_new.astype(jnp.float32))
    return blended.reshape(S_NEW, HEADS_Q * HEAD_DIM).astype(jnp.bfloat16)

def reference(hidden_in, attn_gain, w_query, w_key, w_value, query_gain, key_gain, w_out, cache_keys, cache_values, cache_lengths, slot_request, mlp_gain, w_gate, w_up, w_down, final_gain, w_vocab):
    tokens = hidden_in.astype(jnp.float32)
    normed = norm_rows(tokens, attn_gain).astype(jnp.bfloat16)
    lengths = jnp.take(cache_lengths, slot_request).astype(jnp.int32)
    positions = (lengths[:, None] + jnp.arange(S_NEW, dtype=jnp.int32)[None, :]).astype(jnp.float32)
    queries = jnp.dot(normed, w_query, preferred_element_type=jnp.float32).reshape(REQS, S_NEW, HEADS_Q, HEAD_DIM)
    queries = rotate(norm_rows(queries, query_gain), positions).astype(jnp.bfloat16)
    keys_new = jnp.dot(normed, w_key, preferred_element_type=jnp.float32).reshape(REQS, S_NEW, HEADS_KV, HEAD_DIM)
    keys_new = rotate(norm_rows(keys_new, key_gain), positions).astype(jnp.bfloat16)
    values_new = jnp.dot(normed, w_value, preferred_element_type=jnp.float32).astype(jnp.bfloat16).reshape(REQS, S_NEW, HEADS_KV, HEAD_DIM)
    attended = lax.map(slot_attention, (queries, keys_new, values_new, cache_keys, cache_values, lengths))
    attended = attended.reshape(REQS * S_NEW, HEADS_Q * HEAD_DIM)
    residual = tokens + jnp.dot(attended, w_out, preferred_element_type=jnp.float32)
    mixed_rows = norm_rows(residual, mlp_gain).astype(jnp.bfloat16)
    gate_part = jnp.dot(mixed_rows, w_gate, preferred_element_type=jnp.float32)
    up_part = jnp.dot(mixed_rows, w_up, preferred_element_type=jnp.float32)
    active = (jax.nn.silu(gate_part) * up_part).astype(jnp.bfloat16)
    output = residual + jnp.dot(active, w_down, preferred_element_type=jnp.float32)
    hidden_out = output.astype(jnp.bfloat16)
    last_row = output.reshape(REQS, S_NEW, D)[:, S_NEW - 1, :]
    final_rows = norm_rows(last_row, final_gain).astype(jnp.bfloat16)
    logits = jnp.dot(final_rows, w_vocab, preferred_element_type=jnp.float32)
    row_max = lax.optimization_barrier(jnp.max(logits, axis=1, keepdims=True))
    row_total = lax.optimization_barrier(jnp.sum(jnp.exp(logits - row_max), axis=1, keepdims=True))
    log_probs = logits - row_max - jnp.log(row_total)
    log_probs = jnp.take(log_probs, inverse_order(slot_request), axis=0)
    return (hidden_out, log_probs)
```

```python
import functools
import math

import jax
import jax.numpy as jnp
import numpy as np
from jax import lax
from jax.experimental import pallas as pl
from jax.experimental.pallas import tpu as pltpu
from jax.sharding import PartitionSpec as P

MESH = pl.DeviceIdType.MESH
F32, BF16 = jnp.float32, jnp.bfloat16

D = 2048
HEAD_DIM = 128
ROPE_BASE = 1000000.0
EPS = 1e-06
SHIFT = 4.0
LOG2E = math.log2(math.e)

SIDE = 4
ROWS = 64
HALF = ROWS // 2
PART = HALF // 2
UNITS = 96
PLANE_UNITS = SIDE * UNITS
KEYS = 2048
KEY_BLOCK = 512
VOC = 1187
VOC_BLOCK = 256
N_COPIES = 100


def nt_dot(a, b):
    return lax.dot_general(a, b, (((1,), (1,)), ((), ())), preferred_element_type=F32)


def nn_dot(a, b):
    return jnp.dot(a, b, preferred_element_type=F32)


def step_kernel(
    hidden, attn_gain, query_gain, key_gain, mlp_gain, final_gain, freq, order, order_s, lengths,
    w_query, w_key, w_value, w_out, cache_k, cache_v, w_gate, w_up, w_down, w_vocab,
    out, logp,
    normed, wq, wk, wv, wo, kc, vc, voc, wgu, wd, qs, kn, vn, att, proj, proj_in, gains, resid,
    rows, part, sh1, rh1, sf1, rf1, red, sh2, rh2, sf2, rf2, out_s, out_r,
    fr, final, st1, st2, st3, lsem, ssem, rsem,
):
    req = lax.axis_index("req")
    core = lax.axis_index("head")
    other = 1 - core
    y = req // (SIDE * SIDE)
    x = (req // SIDE) % SIDE
    z = req % SIDE

    def at(yy, xx, zz, cc):
        return ((yy % SIDE) * (SIDE * SIDE) + (xx % SIDE) * SIDE + (zz % SIDE), cc)

    along = {
        "y": lambda d: at(y + d + SIDE, x, z, core),
        "x": lambda d: at(y, x + d + SIDE, z, core),
        "z": lambda d: at(y, x, z + d + SIDE, core),
    }
    sibling = (req, other)
    counters = {"local": 0, "remote": 0}

    def local(src, dst):
        i = counters["local"]
        counters["local"] = i + 1
        return pltpu.make_async_copy(src, dst, lsem.at[i])

    def remote(src, dst, device):
        i = counters["remote"]
        counters["remote"] = i + 1
        return pltpu.make_async_remote_copy(
            src_ref=src, dst_ref=dst, send_sem=ssem.at[i], recv_sem=rsem.at[i],
            device_id=device, device_id_type=MESH,
        )

    sent = []

    def go(copies):
        for c in copies:
            c.start()
            sent.append(c)
        return copies

    def got(copies):
        for c in copies:
            c.wait_recv()

    load_k = local(w_key, wk)
    load_v = local(w_value, wv)
    load_q = local(w_query, wq)
    load_kc = local(cache_k.at[0], kc)
    load_vc = local(cache_v.at[0], vc)
    load_o = local(w_out, wo)
    load_voc = local(w_vocab, voc)

    def shard(zz, h):
        o = pl.multiple_of(zz * UNITS, UNITS)
        return [
            wgu.at[h, pl.ds(o, UNITS)],
            wgu.at[h, pl.ds(PLANE_UNITS + o, UNITS)],
            wd.at[pl.ds(o, UNITS), pl.ds(pl.multiple_of(h * (D // 2), D // 2), D // 2)],
        ]

    def half_shard(zz, h, k):
        n = UNITS // 2
        return [r.at[pl.ds(k * n, n)] for r in shard(zz, h)]

    own = [w_gate, w_up, w_down]
    load_own = [local(s, d) for s, d in zip(own, shard(z, core))]
    load_gain = local(mlp_gain, gains.at[pl.ds(pl.multiple_of(core * 8, 8), 8)])
    for c in [load_k, load_v, load_q]:
        c.start()
    for c in load_own + [load_gain]:
        c.start()

    barrier = pltpu.get_barrier_semaphore()
    peers = [sibling]
    for d in (1, 2, 3):
        peers += [along["x"](d), along["y"](d), at(y, x, z + d, core), at(y, x, z + d, other)]
    for p in peers:
        pl.semaphore_signal(barrier, inc=1, device_id=p, device_id_type=MESH)
    pl.semaphore_wait(barrier, len(peers))

    zc = z
    zm, zp, zo = (z + 3) % SIDE, (z + 1) % SIDE, (z + 2) % SIDE
    w_up1 = go([remote(s, d, along["z"](1)) for s, d in zip(own, shard(zc, core))])
    w_dn1 = go([remote(s, d, along["z"](-1)) for s, d in zip(own, shard(zc, core))])
    gain_x = go([remote(mlp_gain, gains.at[pl.ds(pl.multiple_of(core * 8, 8), 8)], sibling)])
    w_sib = go([remote(s, d, sibling) for s, d in zip(own, shard(zc, core))])
    for c in [load_kc, load_vc, load_o]:
        c.start()

    tokens = hidden[...].astype(F32)
    scale = lax.rsqrt(jnp.mean(tokens * tokens, axis=-1, keepdims=True) + EPS)
    normed[...] = (tokens * scale * attn_gain[...]).astype(BF16)
    slot = order_s[req]
    length = lengths[slot]
    position = (length + lax.broadcasted_iota(jnp.int32, (ROWS, 1), 0)).astype(F32)
    angle = position * freq[...]
    cosine = jnp.cos(angle)
    lane = lax.broadcasted_iota(jnp.int32, (ROWS, HEAD_DIM), 1)
    sine = jnp.where(lane < HEAD_DIM // 2, -jnp.sin(angle), jnp.sin(angle))

    def rotated(v, gain):
        v = v * lax.rsqrt(jnp.mean(v * v, axis=-1, keepdims=True) + EPS) * gain
        return (v * cosine + pltpu.roll(v, HEAD_DIM // 2, 1) * sine).astype(BF16)

    load_k.wait()
    for j in range(2):
        both = nn_dot(normed[...], wk[:, j * 256 : (j + 1) * 256])
        for i in range(2):
            kn[2 * j + i] = rotated(both[:, i * 128 : (i + 1) * 128], key_gain[...])
    load_v.wait()
    for j in range(2):
        vn[:, j * 256 : (j + 1) * 256] = nn_dot(
            normed[...], wv[:, j * 256 : (j + 1) * 256]
        ).astype(BF16)
    load_q.wait()
    for j in range(4):
        both = nn_dot(normed[...], wq[:, j * 256 : (j + 1) * 256])
        for i in range(2):
            qs[j, i * ROWS : (i + 1) * ROWS] = rotated(
                both[:, i * 128 : (i + 1) * 128], query_gain[...]
            )

    load_kc.wait()
    load_vc.wait()
    load_voc.start()
    slope = LOG2E / math.sqrt(HEAD_DIM)
    base = SHIFT * LOG2E
    row_at = lax.broadcasted_iota(jnp.int32, (2 * ROWS, ROWS), 0) % ROWS
    causal = row_at >= lax.broadcasted_iota(jnp.int32, (2 * ROWS, ROWS), 1)

    def one_head(g):
        q = qs[g]
        cols = pl.ds(pl.multiple_of(g * HEAD_DIM, HEAD_DIM), HEAD_DIM)
        fresh = jnp.where(causal, jnp.exp2(nt_dot(q, kn[g]) * slope - base), 0.0)
        total = jnp.sum(fresh, axis=1, keepdims=True)
        acc = nn_dot(fresh.astype(BF16), vn[:, cols])
        for b in range(KEYS // KEY_BLOCK):
            span = slice(b * KEY_BLOCK, (b + 1) * KEY_BLOCK)
            s = nt_dot(q, kc[span, cols])
            key_at = b * KEY_BLOCK + lax.broadcasted_iota(jnp.int32, s.shape, 1)
            p = jnp.where(key_at < length, jnp.exp2(s * slope - base), 0.0)
            total = total + jnp.sum(p, axis=1, keepdims=True)
            acc = acc + nn_dot(p.astype(BF16), vc[span, cols])
        done = (acc / total).astype(BF16)
        att[:, pl.ds(pl.multiple_of(2 * g * HEAD_DIM, HEAD_DIM), HEAD_DIM)] = done[:ROWS]
        att[:, pl.ds(pl.multiple_of((2 * g + 1) * HEAD_DIM, HEAD_DIM), HEAD_DIM)] = done[ROWS:]

    one_head(0)
    one_head(1)

    got(w_up1)
    w_up2 = go([
        remote(r, r, along["z"](1)) for r in half_shard(zm, core, 0)
    ])
    w_sib_m = go([remote(r, r, sibling) for r in shard(zm, core)])
    got(w_dn1)
    w_dn2 = go([
        remote(r, r, along["z"](-1)) for r in half_shard(zp, core, 1)
    ])
    w_sib_p = go([remote(r, r, sibling) for r in shard(zp, core)])

    one_head(2)
    one_head(3)

    load_o.wait()
    for j in range(4):
        cols = slice(j * 512, (j + 1) * 512)
        proj[:, cols] = nn_dot(att[...], wo[:, cols])

    mine = pl.ds(pl.multiple_of(core * HALF, HALF), HALF)
    theirs = pl.ds(pl.multiple_of(other * HALF, HALF), HALF)
    proj_x = go([remote(proj.at[theirs], proj_in, sibling)])
    got(w_up2 + w_dn2)
    w_sib_o = go([remote(r, r, sibling) for r in shard(zo, core)])
    got(gain_x)
    load_gain.wait()
    got(proj_x)
    r = hidden[mine].astype(F32) + (proj[mine] + proj_in[...])
    resid[...] = r
    scale = lax.rsqrt(jnp.mean(r * r, axis=-1, keepdims=True) + EPS)
    for j in range(D // 128):
        cols = slice(j * 128, (j + 1) * 128)
        mixed = (r[:, cols] * scale * gains[j : j + 1]).astype(BF16)
        rows[0, y, x, :, cols] = mixed[:PART]
        rows[1, x, y, :, cols] = mixed[PART:]

    inner, outer = ("x", "y"), ("y", "x")
    inner_at, outer_at = (x, y), (y, x)

    def ring_start(block, p, axis):
        return go([
            remote(block(p), block(p), along[axis](1)),
            remote(block(p), block(p), along[axis](-1)),
        ])

    def ring_pass(block, p, axis, first):
        lo = slice(0, D // 2), slice(D // 2, D)

        def half(pos, k):
            b = block(pos)
            return b.at[..., pl.ds(k * (D // 2), D // 2)]

        got(first[:1])
        a = go([remote(half((p + 3) % SIDE, 0), half((p + 3) % SIDE, 0), along[axis](1))])
        got(first[1:])
        b = go([remote(half((p + 1) % SIDE, 1), half((p + 1) % SIDE, 1), along[axis](-1))])
        return a + b

    def small(s):
        return lambda pos: rows.at[s, outer_at[s], pos]

    def large(s):
        return lambda pos: rows.at[s, pos]

    one = [ring_start(small(s), inner_at[s], inner[s]) for s in range(2)]
    two = [ring_pass(small(s), inner_at[s], inner[s], one[s]) for s in range(2)]
    three = []
    for s in range(2):
        got(two[s])
        three.append(ring_start(large(s), outer_at[s], outer[s]))
    four = [ring_pass(large(s), outer_at[s], outer[s], three[s]) for s in range(2)]

    for c in load_own:
        c.wait()
    got(w_sib + w_sib_m + w_sib_p + w_sib_o)

    def feed(s):
        xa = rows[s].reshape(SIDE * SIDE * PART, D)
        gu = nt_dot(xa[:, : D // 2], wgu[0]) + nt_dot(xa[:, D // 2 :], wgu[1])
        gate, up = gu[:, :PLANE_UNITS], gu[:, PLANE_UNITS:]
        active = (gate / (1.0 + jnp.exp(-gate)) * up).astype(BF16)
        for j in range(4):
            cols = slice(j * 512, (j + 1) * 512)
            part[s, :, :, :, cols] = nn_dot(active, wd[:, cols]).reshape(SIDE, SIDE, PART, 512)

    def reduce_start(s, stage, axis, p, block, sh, rh):
        far = block((p + 2) % SIDE)
        sh[s, 0] = far[..., : D // 2].astype(BF16)
        sh[s, 1] = far[..., D // 2 :].astype(BF16)
        return go([
            remote(sh.at[s, 0], rh.at[s, 0], along[axis](1)),
            remote(sh.at[s, 1], rh.at[s, 1], along[axis](-1)),
        ])

    def reduce_pass(s, axis, p, block, rh, sf, rf, first):
        nxt = block((p + 1) % SIDE)
        prv = block((p + 3) % SIDE)
        sf[s, 0, ..., D // 2 :] = nxt[..., D // 2 :].astype(BF16)
        sf[s, 1, ..., : D // 2] = prv[..., : D // 2].astype(BF16)
        got(first[:1])
        sf[s, 0, ..., : D // 2] = (nxt[..., : D // 2] + rh[s, 0].astype(F32)).astype(BF16)
        a = go([remote(sf.at[s, 0], rf.at[s, 0], along[axis](1))])
        got(first[1:])
        sf[s, 1, ..., D // 2 :] = (prv[..., D // 2 :] + rh[s, 1].astype(F32)).astype(BF16)
        b = go([remote(sf.at[s, 1], rf.at[s, 1], along[axis](-1))])
        return a + b

    def reduce_end(s, p, block, rf, second):
        got(second)
        return block(p) + rf[s, 0].astype(F32) + rf[s, 1].astype(F32)

    def p1(s):
        return lambda pos: part[s, pos]

    def p2(s):
        return lambda pos: red[s, pos]

    five = []
    for s in range(2):
        got(four[s])
        feed(s)
        five.append(reduce_start(s, 1, outer[s], outer_at[s], p1(s), sh1, rh1))
    six = [
        reduce_pass(s, outer[s], outer_at[s], p1(s), rh1, sf1, rf1, five[s]) for s in range(2)
    ]
    seven = []
    for s in range(2):
        red[s] = reduce_end(s, outer_at[s], p1(s), rf1, six[s])
        seven.append(reduce_start(s, 2, inner[s], inner_at[s], p2(s), sh2, rh2))
    eight = [
        reduce_pass(s, inner[s], inner_at[s], p2(s), rh2, sf2, rf2, seven[s]) for s in range(2)
    ]
    for s in range(2):
        span = slice(s * PART, (s + 1) * PART)
        resid[span] = resid[span] + reduce_end(s, inner_at[s], p2(s), rf2, eight[s])

    def slot_rows(first, count):
        return fr.at[pl.ds(pl.multiple_of(first * 16, 16), count * 16)]

    last_z = [remote(slot_rows(x * SIDE + z, 1), slot_rows(x * SIDE + z, 1), along["z"](d)) for d in (1, 2, 3)]
    last_x = [remote(slot_rows(x * SIDE, SIDE), slot_rows(x * SIDE, SIDE), along["x"](d)) for d in (1, 2, 3)]
    last_y = [remote(final.at[y], final.at[y], along["y"](d)) for d in (1, 2, 3)]
    last_c = [remote(final.at[(y + d) % SIDE], final.at[(y + d) % SIDE], sibling) for d in (0, 3, 2, 1)]

    @pl.when(core == 1)
    def _():
        row = resid[HALF - 1 : HALF]
        row = row * lax.rsqrt(jnp.mean(row * row, axis=-1, keepdims=True) + EPS) * final_gain[...]
        row = row.astype(BF16).astype(F32)
        at_row = pl.multiple_of((x * SIDE + z) * 16, 16)
        tile = jnp.concatenate([row[:, j * 128 : (j + 1) * 128] for j in range(16)], axis=0)
        fr[pl.ds(at_row, 16)] = tile
        for c in last_z:
            c.start()
        for c in last_z:
            c.wait()
        for c in last_x:
            c.start()
        for c in last_x:
            c.wait()
        for j in range(16):
            final[y, :, j * 128 : (j + 1) * 128] = fr[pl.ds(j, 16, stride=16)].astype(BF16)
        for c in last_y:
            c.start()
        last_c[0].start()
        for d in (1, 2, 3):
            last_y[d - 1].wait_recv()
            last_c[d].start()
        for c in last_y + last_c:
            c.wait_send()

    keep = pl.ds(pl.multiple_of(core * (D // 2), D // 2), D // 2)
    give = pl.ds(pl.multiple_of(other * (D // 2), D // 2), D // 2)
    out_s[...] = resid[:, give].astype(BF16)
    out_x = go([remote(out_s, out_r, sibling)])
    out[mine] = resid[:, keep].astype(BF16)

    @pl.when(core == 0)
    def _():
        for c in last_c:
            c.wait_recv()

    load_voc.wait()
    pick = (
        order[...] == lax.broadcasted_iota(jnp.int32, (ROWS, ROWS), 0)
    ).astype(BF16)
    final_rows = nn_dot(pick, final[...].reshape(ROWS, D)).astype(BF16)
    top = None
    for start in range(0, VOC, VOC_BLOCK):
        stop = min(start + VOC_BLOCK, VOC)
        part_l = nt_dot(final_rows, voc[start:stop])
        logp[:, start:stop] = part_l
        m = jnp.max(part_l, axis=1, keepdims=True)
        top = m if top is None else jnp.maximum(top, m)
    total = jnp.sum(jnp.exp(logp[...] - top), axis=1, keepdims=True)

    eye = lax.broadcasted_iota(jnp.int32, (ROWS, ROWS), 0) == lax.broadcasted_iota(
        jnp.int32, (ROWS, ROWS), 1
    )

    def as_row(col):
        return jnp.sum(jnp.where(eye, col, 0.0), axis=0, keepdims=True)

    def exchange(buf, index, devices):
        copies = go([remote(buf.at[index], buf.at[index], d) for d in devices])
        got(copies)
        m = jnp.max(buf[:, 0, :ROWS], axis=0, keepdims=True)
        t = jnp.sum(buf[:, 1, :ROWS] * jnp.exp(buf[:, 0, :ROWS] - m), axis=0, keepdims=True)
        return m, t

    def put(buf, index, m, t):
        buf[index, 0:1, :ROWS] = m
        buf[index, 1:2, :ROWS] = t

    put(st1, z * 2 + core, as_row(top), as_row(total))
    m, t = exchange(
        st1, z * 2 + core,
        [sibling] + [at(y, x, z + d, c) for d in (1, 2, 3) for c in (core, other)],
    )
    put(st2, x, m, t)
    m, t = exchange(st2, x, [along["x"](d) for d in (1, 2, 3)])
    put(st3, y, m, t)
    m, t = exchange(st3, y, [along["y"](d) for d in (1, 2, 3)])
    top = jnp.sum(jnp.where(eye, m, 0.0), axis=1, keepdims=True)
    log_total = jnp.sum(jnp.where(eye, jnp.log(t), 0.0), axis=1, keepdims=True)
    logp[...] = logp[...] - top - log_total

    got(out_x)
    out[theirs] = out_r[...]
    for c in sent:
        c.wait_send()


def on_device(
    hidden_in, attn_gain, w_query, w_key, w_value, query_gain, key_gain, w_out,
    cache_keys, cache_values, cache_lengths, slot_request, mlp_gain, w_gate, w_up, w_down,
    final_gain, w_vocab,
):
    half_dim = HEAD_DIM // 2
    one = ROPE_BASE ** (-2.0 * np.arange(half_dim) / HEAD_DIM)
    freq = jnp.asarray(np.concatenate([one, one])[None].astype(np.float32))
    vmem = pl.BlockSpec(memory_space=pltpu.VMEM)
    smem = pl.BlockSpec(memory_space=pltpu.SMEM)
    far = pl.BlockSpec(memory_space=pl.ANY)
    V = pltpu.VMEM
    S = SIDE
    return pl.pallas_call(
        step_kernel,
        out_shape=(
            jax.ShapeDtypeStruct((ROWS, D // 2), BF16),
            jax.ShapeDtypeStruct((ROWS, VOC), F32),
        ),
        in_specs=[vmem] * 8 + [smem] * 2 + [far] * 10,
        out_specs=(vmem, vmem),
        scratch_shapes=[
            V((ROWS, D), BF16),
            V((D, 1024), BF16), V((D, 512), BF16), V((D, 512), BF16), V((1024, D), BF16),
            V((KEYS, 512), BF16), V((KEYS, 512), BF16), V((VOC, D), BF16),
            V((2, 2 * PLANE_UNITS, D // 2), BF16), V((PLANE_UNITS, D), BF16),
            V((4, 2 * ROWS, HEAD_DIM), BF16), V((4, ROWS, HEAD_DIM), BF16), V((ROWS, 512), BF16),
            V((ROWS, 1024), BF16), V((ROWS, D), F32), V((HALF, D), F32), V((16, 128), F32),
            V((HALF, D), F32),
            V((2, S, S, PART, D), BF16), V((2, S, S, PART, D), F32),
            V((2, 2, S, PART, D // 2), BF16), V((2, 2, S, PART, D // 2), BF16),
            V((2, 2, S, PART, D), BF16), V((2, 2, S, PART, D), BF16),
            V((2, S, PART, D), F32),
            V((2, 2, PART, D // 2), BF16), V((2, 2, PART, D // 2), BF16),
            V((2, 2, PART, D), BF16), V((2, 2, PART, D), BF16),
            V((HALF, D // 2), BF16), V((HALF, D // 2), BF16),
            V((S * S * 16, 128), F32), V((S, S * S, D), BF16),
            V((2 * S, 8, 128), F32), V((S, 8, 128), F32), V((S, 8, 128), F32),
            pltpu.SemaphoreType.DMA((16,)),
            pltpu.SemaphoreType.DMA((N_COPIES,)),
            pltpu.SemaphoreType.DMA((N_COPIES,)),
        ],
        compiler_params=pltpu.CompilerParams(
            collective_id=0, has_side_effects=True, vmem_limit_bytes=58 * 1024 * 1024
        ),
    )(
        hidden_in, attn_gain.reshape(1, D), query_gain.reshape(1, HEAD_DIM),
        key_gain.reshape(1, HEAD_DIM), mlp_gain.reshape(8, 128), final_gain.reshape(1, D), freq,
        slot_request.reshape(1, ROWS), slot_request, cache_lengths,
        w_query, w_key, w_value, w_out, cache_keys, cache_values,
        w_gate.T, w_up.T, w_down, w_vocab.T,
    )


def solution(mesh):
    in_specs = (
        P("req", None), P(), P(None, "head"), P(None, "head"), P(None, "head"), P(), P(),
        P("head", None), P("req", None, "head"), P("req", None, "head"), P(), P(), P("head"),
        P("head", "req"), P("head", "req"), P("req", "head"), P(), P(None, ("req", "head")),
    )
    out_specs = (P("req", "head"), P(None, ("req", "head")))
    return jax.shard_map(
        on_device, mesh=mesh, in_specs=in_specs, out_specs=out_specs, check_vma=False
    )
```

```python
import functools
import math

import jax
import jax.numpy as jnp
import numpy as np
from jax import lax
from jax.experimental import pallas as pl
from jax.experimental.pallas import tpu as pltpu
from jax.sharding import PartitionSpec as P

MESH = pl.DeviceIdType.MESH
F32, BF16 = jnp.float32, jnp.bfloat16

D = 2048
HEAD_DIM = 128
ROPE_BASE = 1000000.0
EPS = 1e-06
SHIFT = 4.0
LOG2E = math.log2(math.e)

SIDE = 4
ROWS = 64
HALF = ROWS // 2
PART = HALF // 2
UNITS = 96
PLANE_UNITS = SIDE * UNITS
KEYS = 2048
KEY_BLOCK = 512
VOC = 1187
VOC_BLOCK = 256
N_COPIES = 100


def nt_dot(a, b):
    return lax.dot_general(a, b, (((1,), (1,)), ((), ())), preferred_element_type=F32)


def nn_dot(a, b):
    return jnp.dot(a, b, preferred_element_type=F32)


def step_kernel(
    hidden, attn_gain, query_gain, key_gain, mlp_gain, final_gain, freq, order, order_s, lengths,
    w_query, w_key, w_value, w_out, cache_k, cache_v, w_gate, w_up, w_down, w_vocab,
    out, logp,
    normed, wq, wk, wv, wo, kc, vc, voc, wf, qs, kn, vn, att, proj, proj_in, gains, resid,
    rows, part, in1, mid, in2, out_s, out_r,
    last_a, last_p, last_in, last_b, last_res, spread, last_x, stats,
    lsem, ssem, rsem, gsem, plane_sem, all_sem,
):
    req = lax.axis_index("req")
    core = lax.axis_index("head")
    other = 1 - core
    y = req // (SIDE * SIDE)
    x = (req // SIDE) % SIDE
    z = req % SIDE

    def at(yy, xx, zz, cc):
        return ((yy % SIDE) * (SIDE * SIDE) + (xx % SIDE) * SIDE + (zz % SIDE), cc)

    along = {
        "y": lambda d: at(y + d, x, z, core),
        "x": lambda d: at(y, x + d, z, core),
        "z": lambda d: at(y, x, z + d, core),
    }
    sibling = (req, other)
    counters = {"local": 0, "remote": 0}

    def local(src, dst):
        i = counters["local"]
        counters["local"] = i + 1
        return pltpu.make_async_copy(src, dst, lsem.at[i])

    def remote(src, dst, device):
        i = counters["remote"]
        counters["remote"] = i + 1
        return pltpu.make_async_remote_copy(
            src_ref=src, dst_ref=dst, send_sem=ssem.at[i], recv_sem=rsem.at[i],
            device_id=device, device_id_type=MESH,
        )

    sent = []

    def go(copies):
        for c in copies:
            c.start()
            sent.append(c)
        return copies

    def got(copies):
        for c in copies:
            c.wait_recv()

    load_k = local(w_key, wk)
    load_v = local(w_value, wv)
    load_q = local(w_query, wq)
    load_kc = local(cache_k.at[0], kc)
    load_vc = local(cache_v.at[0], vc)
    load_o = local(w_out, wo)
    load_voc = local(w_vocab, voc)
    unit_at = pl.multiple_of(z * UNITS, UNITS)
    load_own = [
        local(w, wf.at[core, k, pl.ds(unit_at, UNITS)]) for k, w in enumerate((w_gate, w_up, w_down))
    ]
    my_gain = gains.at[pl.ds(pl.multiple_of(core * 8, 8), 8)]
    load_gain = local(mlp_gain, my_gain)
    for c in [load_k, load_v, load_q] + load_own + [load_gain, load_kc, load_vc, load_o]:
        c.start()

    barrier = pltpu.get_barrier_semaphore()
    peers = [sibling]
    for d in (1, 2, 3):
        peers += [along["x"](d), at(y, x + d, z, other), along["y"](d), along["z"](d)]
    for p in peers:
        pl.semaphore_signal(barrier, inc=1, device_id=p, device_id_type=MESH)

    tokens = hidden[...].astype(F32)
    scale = lax.rsqrt(jnp.mean(tokens * tokens, axis=-1, keepdims=True) + EPS)
    normed[...] = (tokens * scale * attn_gain[...]).astype(BF16)
    slot = order_s[req]
    length = lengths[slot]
    position = (length + lax.broadcasted_iota(jnp.int32, (ROWS, 1), 0)).astype(F32)
    angle = position * freq[...]
    cosine = jnp.cos(angle)
    lane = lax.broadcasted_iota(jnp.int32, (ROWS, HEAD_DIM), 1)
    sine = jnp.where(lane < HEAD_DIM // 2, -jnp.sin(angle), jnp.sin(angle))

    def rotated(v, gain):
        v = v * lax.rsqrt(jnp.mean(v * v, axis=-1, keepdims=True) + EPS) * gain
        return (v * cosine + pltpu.roll(v, HEAD_DIM // 2, 1) * sine).astype(BF16)

    load_k.wait()
    for j in range(2):
        both = nn_dot(normed[...], wk[:, j * 256 : (j + 1) * 256])
        for i in range(2):
            kn[2 * j + i] = rotated(both[:, i * 128 : (i + 1) * 128], key_gain[...])
    load_v.wait()
    for j in range(2):
        vn[:, j * 256 : (j + 1) * 256] = nn_dot(
            normed[...], wv[:, j * 256 : (j + 1) * 256]
        ).astype(BF16)

    def shard(zz, h):
        return wf.at[h, :, pl.ds(pl.multiple_of(zz * UNITS, UNITS), UNITS)]

    def half_shard(zz, h, k):
        n = UNITS // 2
        return wf.at[h, :, pl.ds(pl.multiple_of(zz * UNITS + k * n, n), n)]

    zm, zp, zo = (z + 3) % SIDE, (z + 1) % SIDE, (z + 2) % SIDE
    for c in load_own + [load_gain]:
        c.wait()
    pl.semaphore_wait(barrier, len(peers))
    w_first, w_second = [], []
    for copies, k_up in ((w_first, 0), (w_second, 1)):
        copies += go([
            remote(half_shard(z, core, k_up), half_shard(z, core, k_up), along["z"](1)),
            remote(half_shard(z, core, 1 - k_up), half_shard(z, core, 1 - k_up), along["z"](-1)),
        ])
    gain_x = go([remote(my_gain, my_gain, sibling)])
    w_sib = go([remote(shard(z, core), shard(z, core), sibling)])
    for d in (1, 2, 3):
        pl.semaphore_signal(plane_sem, inc=1, device_id=along["y"](d), device_id_type=MESH)

    load_q.wait()
    for j in range(4):
        both = nn_dot(normed[...], wq[:, j * 256 : (j + 1) * 256])
        for i in range(2):
            qs[j, i * ROWS : (i + 1) * ROWS] = rotated(
                both[:, i * 128 : (i + 1) * 128], query_gain[...]
            )

    load_kc.wait()
    load_vc.wait()
    load_voc.start()
    slope = LOG2E / math.sqrt(HEAD_DIM)
    base = SHIFT * LOG2E
    row_at = lax.broadcasted_iota(jnp.int32, (2 * ROWS, ROWS), 0) % ROWS
    causal = row_at >= lax.broadcasted_iota(jnp.int32, (2 * ROWS, ROWS), 1)

    def one_head(g):
        q = qs[g]
        cols = slice(g * HEAD_DIM, (g + 1) * HEAD_DIM)
        fresh = jnp.where(causal, jnp.exp2(nt_dot(q, kn[g]) * slope - base), 0.0)
        total = jnp.sum(fresh, axis=1, keepdims=True)
        acc = nn_dot(fresh.astype(BF16), vn[:, cols])
        for b in range(KEYS // KEY_BLOCK):
            span = slice(b * KEY_BLOCK, (b + 1) * KEY_BLOCK)
            s = nt_dot(q, kc[span, cols])
            key_at = b * KEY_BLOCK + lax.broadcasted_iota(jnp.int32, s.shape, 1)
            p = jnp.where(key_at < length, jnp.exp2(s * slope - base), 0.0)
            total = total + jnp.sum(p, axis=1, keepdims=True)
            acc = acc + nn_dot(p.astype(BF16), vc[span, cols])
        done = (acc / total).astype(BF16)
        att[:, 2 * g * HEAD_DIM : (2 * g + 1) * HEAD_DIM] = done[:ROWS]
        att[:, (2 * g + 1) * HEAD_DIM : (2 * g + 2) * HEAD_DIM] = done[ROWS:]

    for g in range(4):
        one_head(g)

    load_o.wait()
    for j in range(4):
        cols = slice(j * 512, (j + 1) * 512)
        proj[:, cols] = nn_dot(att[...], wo[:, cols])
    mine = pl.ds(pl.multiple_of(core * HALF, HALF), HALF)
    theirs = pl.ds(pl.multiple_of(other * HALF, HALF), HALF)
    proj_x = go([remote(proj.at[theirs], proj_in, sibling)])
    pl.semaphore_wait(plane_sem, 3)
    for d in (1, 2, 3):
        pl.semaphore_signal(all_sem, inc=1, device_id=along["z"](d), device_id_type=MESH)
    got(gain_x + proj_x)
    r = hidden[mine].astype(F32) + (proj[mine] + proj_in[...])
    resid[...] = r
    scale = lax.rsqrt(jnp.mean(r * r, axis=-1, keepdims=True) + EPS)
    for j in range(D // 128):
        cols = slice(j * 128, (j + 1) * 128)
        mixed = (r[:, cols] * scale * gains[j : j + 1]).astype(BF16)
        rows[0, y, x, :, cols] = mixed[:PART]
        rows[1, x, y, :, cols] = mixed[PART:]

    inner, outer = ("x", "y"), ("y", "x")
    inner_at, outer_at = (x, y), (y, x)
    hops = (2, 1, 3)

    def piece(s, o, i):
        return rows.at[s, o % SIDE, i % SIDE]

    def push(s, i, axis):
        b = piece(s, outer_at[s], i)
        return {d: go([remote(b, b, along[axis](d))])[0] for d in hops}

    one = [push(s, inner_at[s], inner[s]) for s in range(2)]
    two = [{0: push(s, inner_at[s], outer[s])} for s in range(2)]

    def each_chip(body):
        def step(d, carry):
            body(lax.rem(req + d, SIDE * SIDE * SIDE))
            return carry

        lax.fori_loop(1, SIDE**3, step, 0)

    def all_but_one(buf, n, k):
        return pltpu.make_async_remote_copy(
            src_ref=buf.at[pl.ds(0, n)], dst_ref=buf.at[pl.ds(0, n)],
            send_sem=gsem.at[k], recv_sem=gsem.at[k + 1], device_id=sibling, device_id_type=MESH,
        )

    def to_chip(src, dst, q, k):
        pltpu.make_async_remote_copy(
            src_ref=src, dst_ref=dst, send_sem=gsem.at[k], recv_sem=gsem.at[k + 1],
            device_id=(q, core), device_id_type=MESH,
        ).start()

    pl.semaphore_wait(all_sem, 3)
    chips = SIDE**3

    @pl.when(core == 1)
    def _():
        tile = jnp.concatenate(
            [resid[HALF - 1 : HALF, j * 128 : (j + 1) * 128] for j in range(16)], axis=0
        )
        last_res[...] = tile
        power = jnp.sum(jnp.sum(tile * tile, axis=1, keepdims=True), axis=0, keepdims=True)
        last_a[req] = (tile * lax.rsqrt(power / D + EPS) * gains[...]).astype(BF16)
        each_chip(lambda q: to_chip(last_a.at[req], last_a.at[req], q, 0))

    got(w_first)
    w_on = go([
        remote(half_shard(zm, core, 0), half_shard(zm, core, 0), along["z"](1)),
        remote(half_shard(zp, core, 1), half_shard(zp, core, 1), along["z"](-1)),
    ])

    for d in (1, 3, 2):
        for s in range(2):
            one[s][d].wait_recv()
            two[s][d] = push(s, inner_at[s] - d + SIDE, outer[s])
    got(w_second)
    w_sib += go([remote(shard(zm, core), shard(zm, core), sibling)])
    w_sib += go([remote(shard(zp, core), shard(zp, core), sibling)])

    def unpack(tiles):
        spread[...] = tiles[...].astype(F32).reshape(chips * 16, 128)
        for j in range(16):
            last_x[:, j * 128 : (j + 1) * 128] = spread[pl.ds(j, chips, stride=16)].astype(BF16)

    got(w_sib[:1])

    @pl.when(core == 1)
    def _():
        all_but_one(last_a, chips - 1, 0).wait_recv()
        unpack(last_a)
        units = pl.ds(unit_at, UNITS)
        lo, hi = last_x[:, : D // 2], last_x[:, D // 2 :]
        gate = nt_dot(lo, wf[0, 0, units]) + nt_dot(hi, wf[1, 0, units])
        up = nt_dot(lo, wf[0, 1, units]) + nt_dot(hi, wf[1, 1, units])
        active = (gate / (1.0 + jnp.exp(-gate)) * up).astype(BF16)
        for h in range(2):
            down = nn_dot(active, wf[h, 2, units])
            for j in range(8):
                spread[pl.ds(8 * h + j, chips, stride=16)] = down[:, j * 128 : (j + 1) * 128]
        last_p[...] = spread[...].reshape(chips, 16, 128).astype(BF16)
        last_in[req] = last_p[req]
        each_chip(lambda q: to_chip(last_p.at[q], last_in.at[req], q, 2))

    got(w_on)
    w_sib += go([remote(shard(zo, core), shard(zo, core), sibling)])

    last_c = remote(last_b.at[req], last_b.at[req], sibling)

    @pl.when(core == 1)
    def _():
        all_but_one(last_in, chips - 1, 2).wait_recv()
        tile = last_res[...] + jnp.sum(last_in[...].astype(F32), axis=0)
        power = jnp.sum(jnp.sum(tile * tile, axis=1, keepdims=True), axis=0, keepdims=True)
        last_b[req] = (tile * lax.rsqrt(power / D + EPS) * final_gain[...]).astype(BF16)
        last_c.start()
        last_c.wait_send()

    @pl.when(core == 0)
    def _():
        last_c.wait_recv()

    each_chip(lambda q: to_chip(last_b.at[req], last_b.at[req], q, 4))

    got(w_sib[1:])

    def feed(s):
        xa = rows[s].reshape(SIDE * SIDE * PART, D)
        gu = nt_dot(xa[:, : D // 2], wf[0, 0:2].reshape(2 * PLANE_UNITS, D // 2))
        gu += nt_dot(xa[:, D // 2 :], wf[1, 0:2].reshape(2 * PLANE_UNITS, D // 2))
        gate, up = gu[:, :PLANE_UNITS], gu[:, PLANE_UNITS:]
        active = (gate / (1.0 + jnp.exp(-gate)) * up).astype(BF16)
        for j in range(4):
            down = nn_dot(active, wf[j // 2, 2, :, (j % 2) * 512 : (j % 2 + 1) * 512])
            part[s, :, :, :, j * 512 : (j + 1) * 512] = down.astype(BF16).reshape(
                SIDE, SIDE, PART, 512
            )

    back = [{}, {}]
    near = (2, 1, 3, 0)
    for s in range(2):
        for k in (0, 1, 3, 2):
            got([two[s][k][d] for d in (1, 3, 2)])
        feed(s)
        for k in near:
            i = (inner_at[s] + k) % SIDE
            back[s][k] = go([
                remote(
                    part.at[s, (outer_at[s] + d) % SIDE, i], in1.at[s, d - 1, k],
                    along[outer[s]](d),
                )
                for d in hops
            ])

    all_but_one(last_b, chips - 1, 4).wait_recv()
    unpack(last_b)
    load_voc.wait()
    pick = (
        order[...] == lax.broadcasted_iota(jnp.int32, (ROWS, ROWS), 0)
    ).astype(BF16)
    final_rows = nn_dot(pick, last_x[...]).astype(BF16)
    top = None
    for start in range(0, VOC, VOC_BLOCK):
        stop = min(start + VOC_BLOCK, VOC)
        block = nt_dot(final_rows, voc[start:stop])
        logp[:, start:stop] = block
        m = jnp.max(block, axis=1, keepdims=True)
        top = m if top is None else jnp.maximum(top, m)
    total = jnp.sum(jnp.exp(logp[...] - top), axis=1, keepdims=True)
    eye = lax.broadcasted_iota(jnp.int32, (ROWS, ROWS), 0) == lax.broadcasted_iota(
        jnp.int32, (ROWS, ROWS), 1
    )

    def as_row(col):
        return jnp.sum(jnp.where(eye, col, 0.0), axis=0, keepdims=True)

    me = req * 2 + core
    stats[me] = jnp.concatenate([as_row(top), as_row(total)], axis=1)

    def tell(d, carry):
        q = lax.rem(me + d, 2 * chips)
        pltpu.make_async_remote_copy(
            src_ref=stats.at[me], dst_ref=stats.at[me], send_sem=gsem.at[6], recv_sem=gsem.at[7],
            device_id=(q // 2, q % 2), device_id_type=MESH,
        ).start()
        return carry

    lax.fori_loop(1, 2 * chips, tell, 0)

    ends = [{}, {}]
    keep = [None, None]
    for k in near:
        for s in range(2):
            got(back[s][k])
            i = (inner_at[s] + k) % SIDE
            tot = part[s, outer_at[s], i].astype(F32)
            for d in range(3):
                tot += in1[s, d, k].astype(F32)
            if k == 0:
                keep[s] = tot
            else:
                mid[s, k - 1] = tot.astype(BF16)
                ends[s][k] = go([remote(mid.at[s, k - 1], in2.at[s, k - 1], along[inner[s]](k))])[0]
    for s in range(2):
        span = slice(s * PART, (s + 1) * PART)
        resid[span] = resid[span] + keep[s]

    all_but_one(stats, 2 * chips - 1, 6).wait_recv()
    tops = stats[:, 0, :ROWS]
    m = jnp.max(tops, axis=0, keepdims=True)
    t = jnp.sum(stats[:, 0, ROWS:] * jnp.exp(tops - m), axis=0, keepdims=True)
    top = jnp.sum(jnp.where(eye, m, 0.0), axis=1, keepdims=True)
    log_total = jnp.sum(jnp.where(eye, jnp.log(t), 0.0), axis=1, keepdims=True)
    logp[...] = logp[...] - top - log_total

    for s in range(2):
        got([ends[s][k] for k in (2, 1, 3)])
        span = slice(s * PART, (s + 1) * PART)
        tot = resid[span]
        for d in range(3):
            tot += in2[s, d].astype(F32)
        resid[span] = tot
    stay = pl.ds(pl.multiple_of(core * (D // 2), D // 2), D // 2)
    give = pl.ds(pl.multiple_of(other * (D // 2), D // 2), D // 2)
    out_s[...] = resid[:, give].astype(BF16)
    out_x = go([remote(out_s, out_r, sibling)])
    out[mine] = resid[:, stay].astype(BF16)

    @pl.when(core == 1)
    def _():
        all_but_one(last_a, chips - 1, 0).wait_send()
        all_but_one(last_p, chips - 1, 2).wait_send()

    all_but_one(last_b, chips - 1, 4).wait_send()
    all_but_one(stats, 2 * chips - 1, 6).wait_send()
    for c in sent[:-1]:
        c.wait_send()
    got(out_x)
    out[theirs] = out_r[...]
    out_x[0].wait_send()


def copy_kernel(a, b, a_out, b_out, sem):
    copies = [
        pltpu.make_async_copy(a, a_out, sem.at[0]),
        pltpu.make_async_copy(b, b_out, sem.at[1]),
    ]
    for c in copies:
        c.start()
    for c in copies:
        c.wait()


def on_device(
    hidden_in, attn_gain, w_query, w_key, w_value, query_gain, key_gain, w_out,
    cache_keys, cache_values, cache_lengths, slot_request, mlp_gain, w_gate, w_up, w_down,
    final_gain, w_vocab,
):
    half_dim = HEAD_DIM // 2
    one = ROPE_BASE ** (-2.0 * np.arange(half_dim) / HEAD_DIM)
    freq = jnp.asarray(np.concatenate([one, one])[None].astype(np.float32))
    vmem = pl.BlockSpec(memory_space=pltpu.VMEM)
    smem = pl.BlockSpec(memory_space=pltpu.SMEM)
    far = pl.BlockSpec(memory_space=pl.ANY)
    V = pltpu.VMEM
    S = SIDE
    results = (
        jax.ShapeDtypeStruct((ROWS, D // 2), BF16),
        jax.ShapeDtypeStruct((ROWS, VOC), F32),
    )
    out, logp = pl.pallas_call(
        step_kernel,
        out_shape=results,
        in_specs=[vmem] * 8 + [smem] * 2 + [far] * 10,
        out_specs=(vmem, vmem),
        scratch_shapes=[
            V((ROWS, D), BF16),
            V((D, 1024), BF16), V((D, 512), BF16), V((D, 512), BF16), V((1024, D), BF16),
            V((KEYS, 512), BF16), V((KEYS, 512), BF16), V((VOC, D), BF16),
            V((2, 3, PLANE_UNITS, D // 2), BF16),
            V((4, 2 * ROWS, HEAD_DIM), BF16), V((4, ROWS, HEAD_DIM), BF16), V((ROWS, 512), BF16),
            V((ROWS, 1024), BF16), V((ROWS, D), F32), V((HALF, D), F32), V((16, 128), F32),
            V((HALF, D), F32),
            V((2, S, S, PART, D), BF16), V((2, S, S, PART, D), BF16),
            V((2, 3, S, PART, D), BF16), V((2, 3, PART, D), BF16), V((2, 3, PART, D), BF16),
            V((HALF, D // 2), BF16), V((HALF, D // 2), BF16),
            V((S**3, 16, 128), BF16), V((S**3, 16, 128), BF16), V((S**3, 16, 128), BF16),
            V((S**3, 16, 128), BF16), V((16, 128), F32), V((S**3 * 16, 128), F32),
            V((S**3, D), BF16), V((2 * S**3, 1, 128), F32),
            pltpu.SemaphoreType.DMA((16,)),
            pltpu.SemaphoreType.DMA((N_COPIES,)),
            pltpu.SemaphoreType.DMA((N_COPIES,)),
            pltpu.SemaphoreType.DMA((8,)),
            pltpu.SemaphoreType.REGULAR,
            pltpu.SemaphoreType.REGULAR,
        ],
        compiler_params=pltpu.CompilerParams(
            collective_id=0, has_side_effects=True, vmem_limit_bytes=58 * 1024 * 1024
        ),
    )(
        hidden_in, attn_gain.reshape(1, D), query_gain.reshape(1, HEAD_DIM),
        key_gain.reshape(1, HEAD_DIM), mlp_gain.reshape(8, 128), final_gain.reshape(16, 128), freq,
        slot_request.reshape(1, ROWS), slot_request, cache_lengths,
        w_query, w_key, w_value, w_out, cache_keys, cache_values,
        w_gate.T, w_up.T, w_down, w_vocab.T,
    )
    return pl.pallas_call(
        copy_kernel,
        out_shape=results,
        in_specs=[far] * 2,
        out_specs=(far, far),
        scratch_shapes=[pltpu.SemaphoreType.DMA((2,))],
    )(out, logp)


def solution(mesh):
    in_specs = (
        P("req", None), P(), P(None, "head"), P(None, "head"), P(None, "head"), P(), P(),
        P("head", None), P("req", None, "head"), P("req", None, "head"), P(), P(), P("head"),
        P("head", "req"), P("head", "req"), P("req", "head"), P(), P(None, ("req", "head")),
    )
    out_specs = (P("req", "head"), P(None, ("req", "head")))
    return jax.shard_map(
        on_device, mesh=mesh, in_specs=in_specs, out_specs=out_specs, check_vma=False
    )
```

```python
import functools
import math

import jax
import jax.numpy as jnp
import numpy as np
from jax import lax
from jax.experimental import pallas as pl
from jax.experimental.pallas import tpu as pltpu
from jax.sharding import PartitionSpec as P

MESH = pl.DeviceIdType.MESH
F32, BF16 = jnp.float32, jnp.bfloat16

D = 2048
HEAD_DIM = 128
ROPE_BASE = 1000000.0
EPS = 1e-06
SHIFT = 4.0
LOG2E = math.log2(math.e)

SIDE = 4
ROWS = 64
HALF = ROWS // 2
PART = HALF // 2
UNITS = 96
PLANE_UNITS = SIDE * UNITS
KEYS = 2048
KEY_BLOCK = 1024
VOC = 1187
VOC_BLOCK = 256
N_COPIES = 100


def nt_dot(a, b):
    return lax.dot_general(a, b, (((1,), (1,)), ((), ())), preferred_element_type=F32)


def nn_dot(a, b):
    return jnp.dot(a, b, preferred_element_type=F32)


def step_kernel(
    hidden, attn_gain, query_gain, key_gain, mlp_gain, final_gain, freq, order, order_s, lengths,
    w_query, w_key, w_value, w_out, cache_k, cache_v, w_gate, w_up, w_down, w_vocab,
    out_hbm, logp_hbm,
    out, logp, normed, wq, wk, wv, wo, kc, vc, voc, wf, qs, kn, vn, att, proj, proj_in, gains, resid,
    rows, part, in1, mid, in2, out_s, out_r,
    last_a, last_p, last_in, last_b, last_res, spread, last_x, stats,
    lsem, ssem, rsem, gsem, plane_sem, all_sem,
):
    req = lax.axis_index("req")
    core = lax.axis_index("head")
    other = 1 - core
    y = req // (SIDE * SIDE)
    x = (req // SIDE) % SIDE
    z = req % SIDE

    def at(yy, xx, zz, cc):
        return ((yy % SIDE) * (SIDE * SIDE) + (xx % SIDE) * SIDE + (zz % SIDE), cc)

    along = {
        "y": lambda d: at(y + d, x, z, core),
        "x": lambda d: at(y, x + d, z, core),
        "z": lambda d: at(y, x, z + d, core),
    }
    sibling = (req, other)
    counters = {"local": 0, "remote": 0}

    def local(src, dst):
        i = counters["local"]
        counters["local"] = i + 1
        return pltpu.make_async_copy(src, dst, lsem.at[i])

    def remote(src, dst, device):
        i = counters["remote"]
        counters["remote"] = i + 1
        return pltpu.make_async_remote_copy(
            src_ref=src, dst_ref=dst, send_sem=ssem.at[i], recv_sem=rsem.at[i],
            device_id=device, device_id_type=MESH,
        )

    sent = []

    def go(copies):
        for c in copies:
            c.start()
            sent.append(c)
        return copies

    def got(copies):
        for c in copies:
            c.wait_recv()

    def load(src, dst, parts):
        n = src.shape[0] // parts
        return [local(src.at[pl.ds(k * n, n)], dst.at[pl.ds(k * n, n)]) for k in range(parts)]

    def begin(copies):
        for c in copies:
            c.start()

    def done_with(copies):
        for c in copies:
            c.wait()

    load_k = load(w_key, wk, 2)
    load_v = load(w_value, wv, 2)
    load_q = load(w_query, wq, 4)
    load_kc = load(cache_k.at[0], kc, 2)
    load_vc = load(cache_v.at[0], vc, 2)
    load_o = load(w_out, wo, 4)
    load_voc = [local(w_vocab, voc)]
    unit_at = pl.multiple_of(z * UNITS, UNITS)
    load_own = [
        local(w, wf.at[core, k, pl.ds(unit_at, UNITS)]) for k, w in enumerate((w_gate, w_up, w_down))
    ]
    my_gain = gains.at[pl.ds(pl.multiple_of(core * 8, 8), 8)]
    load_gain = local(mlp_gain, my_gain)
    begin(load_own + [load_gain] + load_k + load_v + load_q + load_kc + load_vc + load_o)

    barrier = pltpu.get_barrier_semaphore()
    peers = [sibling]
    for d in (1, 2, 3):
        peers += [along["x"](d), at(y, x + d, z, other), along["y"](d), along["z"](d)]
    for p in peers:
        pl.semaphore_signal(barrier, inc=1, device_id=p, device_id_type=MESH)

    def shard(zz, h):
        return wf.at[h, :, pl.ds(pl.multiple_of(zz * UNITS, UNITS), UNITS)]

    def half_shard(zz, h, k):
        n = UNITS // 2
        return wf.at[h, :, pl.ds(pl.multiple_of(zz * UNITS + k * n, n), n)]

    zm, zp, zo = (z + 3) % SIDE, (z + 1) % SIDE, (z + 2) % SIDE
    done_with(load_own + [load_gain])
    pl.semaphore_wait(barrier, len(peers))
    w_first, w_second = [], []
    for copies, k_up in ((w_first, 0), (w_second, 1)):
        copies += go([
            remote(half_shard(z, core, k_up), half_shard(z, core, k_up), along["z"](1)),
            remote(half_shard(z, core, 1 - k_up), half_shard(z, core, 1 - k_up), along["z"](-1)),
        ])
    gain_x = go([remote(my_gain, my_gain, sibling)])
    w_sib = go([remote(shard(z, core), shard(z, core), sibling)])
    for d in (1, 2, 3):
        pl.semaphore_signal(plane_sem, inc=1, device_id=along["y"](d), device_id_type=MESH)

    tokens = hidden[...].astype(F32)
    scale = lax.rsqrt(jnp.mean(tokens * tokens, axis=-1, keepdims=True) + EPS)
    normed[...] = (tokens * scale * attn_gain[...]).astype(BF16)
    slot = order_s[req]
    length = lengths[slot]
    position = (length + lax.broadcasted_iota(jnp.int32, (ROWS, 1), 0)).astype(F32)
    angle = position * freq[...]
    cosine = jnp.cos(angle)
    lane = lax.broadcasted_iota(jnp.int32, (ROWS, HEAD_DIM), 1)
    sine = jnp.where(lane < HEAD_DIM // 2, -jnp.sin(angle), jnp.sin(angle))

    def rotated(v, gain):
        v = v * lax.rsqrt(jnp.mean(v * v, axis=-1, keepdims=True) + EPS) * gain
        return (v * cosine + pltpu.roll(v, HEAD_DIM // 2, 1) * sine).astype(BF16)

    done_with(load_k)
    for j in range(2):
        both = nn_dot(normed[...], wk[:, j * 256 : (j + 1) * 256])
        for i in range(2):
            kn[2 * j + i] = rotated(both[:, i * 128 : (i + 1) * 128], key_gain[...])
    done_with(load_v)
    for j in range(2):
        vn[:, j * 256 : (j + 1) * 256] = nn_dot(
            normed[...], wv[:, j * 256 : (j + 1) * 256]
        ).astype(BF16)

    done_with(load_q)
    for j in range(4):
        both = nn_dot(normed[...], wq[:, j * 256 : (j + 1) * 256])
        for i in range(2):
            qs[j, i * ROWS : (i + 1) * ROWS] = rotated(
                both[:, i * 128 : (i + 1) * 128], query_gain[...]
            )

    done_with(load_kc)
    done_with(load_vc)
    begin(load_voc)
    slope = LOG2E / math.sqrt(HEAD_DIM)
    base = SHIFT * LOG2E
    row_at = lax.broadcasted_iota(jnp.int32, (2 * ROWS, ROWS), 0) % ROWS
    causal = row_at >= lax.broadcasted_iota(jnp.int32, (2 * ROWS, ROWS), 1)

    def one_head(g):
        q = qs[g]
        cols = slice(g * HEAD_DIM, (g + 1) * HEAD_DIM)
        fresh = jnp.where(causal, jnp.exp2(nt_dot(q, kn[g]) * slope - base), 0.0)
        total = jnp.sum(fresh, axis=1, keepdims=True)
        acc = nn_dot(fresh.astype(BF16), vn[:, cols])
        for b in range(KEYS // KEY_BLOCK):
            span = slice(b * KEY_BLOCK, (b + 1) * KEY_BLOCK)
            s = nt_dot(q, kc[span, cols])
            key_at = b * KEY_BLOCK + lax.broadcasted_iota(jnp.int32, s.shape, 1)
            p = jnp.where(key_at < length, jnp.exp2(s * slope - base), 0.0)
            total = total + jnp.sum(p, axis=1, keepdims=True)
            acc = acc + nn_dot(p.astype(BF16), vc[span, cols])
        done = (acc / total).astype(BF16)
        att[:, 2 * g * HEAD_DIM : (2 * g + 1) * HEAD_DIM] = done[:ROWS]
        att[:, (2 * g + 1) * HEAD_DIM : (2 * g + 2) * HEAD_DIM] = done[ROWS:]

    for g in range(4):
        one_head(g)

    done_with(load_o)
    for j in range(4):
        cols = slice(j * 512, (j + 1) * 512)
        proj[:, cols] = nn_dot(att[...], wo[:, cols])
    mine = pl.ds(pl.multiple_of(core * HALF, HALF), HALF)
    theirs = pl.ds(pl.multiple_of(other * HALF, HALF), HALF)
    proj_x = go([remote(proj.at[theirs], proj_in, sibling)])
    pl.semaphore_wait(plane_sem, 3)
    for d in (1, 2, 3):
        pl.semaphore_signal(all_sem, inc=1, device_id=along["z"](d), device_id_type=MESH)
    got(gain_x + proj_x)
    r = hidden[mine].astype(F32) + (proj[mine] + proj_in[...])
    resid[...] = r
    scale = lax.rsqrt(jnp.mean(r * r, axis=-1, keepdims=True) + EPS)
    for j in range(D // 128):
        cols = slice(j * 128, (j + 1) * 128)
        mixed = (r[:, cols] * scale * gains[j : j + 1]).astype(BF16)
        rows[0, y, x, :, cols] = mixed[:PART]
        rows[1, x, y, :, cols] = mixed[PART:]

    inner, outer = ("x", "y"), ("y", "x")
    inner_at, outer_at = (x, y), (y, x)
    hops = (1, 3, 2)

    def piece(s, o, i):
        return rows.at[s, o % SIDE, i % SIDE]

    def push(s, i, axis):
        b = piece(s, outer_at[s], i)
        return {d: go([remote(b, b, along[axis](d))])[0] for d in hops}

    def each_chip(body):
        def step(d, carry):
            body(lax.rem(req + d, SIDE * SIDE * SIDE))
            return carry

        lax.fori_loop(1, SIDE**3, step, 0)

    def all_but_one(buf, n, k):
        return pltpu.make_async_remote_copy(
            src_ref=buf.at[pl.ds(0, n)], dst_ref=buf.at[pl.ds(0, n)],
            send_sem=gsem.at[k], recv_sem=gsem.at[k + 1], device_id=sibling, device_id_type=MESH,
        )

    def to_chip(src, dst, q, k):
        pltpu.make_async_remote_copy(
            src_ref=src, dst_ref=dst, send_sem=gsem.at[k], recv_sem=gsem.at[k + 1],
            device_id=(q, core), device_id_type=MESH,
        ).start()

    pl.semaphore_wait(all_sem, 3)
    chips = SIDE**3

    @pl.when(core == 1)
    def _():
        tile = jnp.concatenate(
            [resid[HALF - 1 : HALF, j * 128 : (j + 1) * 128] for j in range(16)], axis=0
        )
        last_res[...] = tile
        power = jnp.sum(jnp.sum(tile * tile, axis=1, keepdims=True), axis=0, keepdims=True)
        last_a[req] = (tile * lax.rsqrt(power / D + EPS) * gains[...]).astype(BF16)
        each_chip(lambda q: to_chip(last_a.at[req], last_a.at[req], q, 0))

    one = [push(s, inner_at[s], inner[s]) for s in range(2)]
    two = [{0: push(s, inner_at[s], outer[s])} for s in range(2)]
    got(w_first)
    w_on = go([
        remote(half_shard(zm, core, 0), half_shard(zm, core, 0), along["z"](1)),
        remote(half_shard(zp, core, 1), half_shard(zp, core, 1), along["z"](-1)),
    ])

    def unpack(tiles):
        spread[...] = tiles[...].astype(F32).reshape(chips * 16, 128)
        for j in range(16):
            last_x[:, j * 128 : (j + 1) * 128] = spread[pl.ds(j, chips, stride=16)].astype(BF16)

    got(w_sib[:1])

    @pl.when(core == 1)
    def _():
        all_but_one(last_a, chips - 1, 0).wait_recv()
        unpack(last_a)
        units = pl.ds(unit_at, UNITS)
        lo, hi = last_x[:, : D // 2], last_x[:, D // 2 :]
        gate = nt_dot(lo, wf[0, 0, units]) + nt_dot(hi, wf[1, 0, units])
        up = nt_dot(lo, wf[0, 1, units]) + nt_dot(hi, wf[1, 1, units])
        active = (gate / (1.0 + jnp.exp(-gate)) * up).astype(BF16)
        for h in range(2):
            down = nn_dot(active, wf[h, 2, units])
            for j in range(8):
                spread[pl.ds(8 * h + j, chips, stride=16)] = down[:, j * 128 : (j + 1) * 128]
        last_p[...] = spread[...].reshape(chips, 16, 128).astype(BF16)
        last_in[req] = last_p[req]
        each_chip(lambda q: to_chip(last_p.at[q], last_in.at[req], q, 2))

    for d in (1, 3, 2):
        for s in range(2):
            one[s][d].wait_recv()
            two[s][d] = push(s, inner_at[s] - d + SIDE, outer[s])

    got(w_second)
    w_sib += go([remote(shard(zm, core), shard(zm, core), sibling)])
    w_sib += go([remote(shard(zp, core), shard(zp, core), sibling)])
    got(w_on)
    w_sib += go([remote(shard(zo, core), shard(zo, core), sibling)])

    last_c = remote(last_b.at[req], last_b.at[req], sibling)

    def tell_final():
        each_chip(lambda q: to_chip(last_b.at[req], last_b.at[req], q, 4))

    @pl.when(core == 1)
    def _():
        all_but_one(last_in, chips - 1, 2).wait_recv()
        tile = last_res[...] + jnp.sum(last_in[...].astype(F32), axis=0)
        power = jnp.sum(jnp.sum(tile * tile, axis=1, keepdims=True), axis=0, keepdims=True)
        last_b[req] = (tile * lax.rsqrt(power / D + EPS) * final_gain[...]).astype(BF16)
        last_c.start()
        tell_final()
        last_c.wait_send()

    got(w_sib[1:])
    block_rows = SIDE * PART

    def feed(k):
        own = [(outer_at[s] + k) % SIDE for s in range(2)]
        xa = jnp.concatenate([rows[s, own[s]].reshape(block_rows, D) for s in range(2)], axis=0)
        gu = nt_dot(xa[:, : D // 2], wf[0, 0:2].reshape(2 * PLANE_UNITS, D // 2))
        gu += nt_dot(xa[:, D // 2 :], wf[1, 0:2].reshape(2 * PLANE_UNITS, D // 2))
        gate, up = gu[:, :PLANE_UNITS], gu[:, PLANE_UNITS:]
        active = (gate / (1.0 + jnp.exp(-gate)) * up).astype(BF16)
        for j in range(4):
            down = nn_dot(active, wf[j // 2, 2, :, (j % 2) * 512 : (j % 2 + 1) * 512])
            down = down.astype(BF16).reshape(2, SIDE, PART, 512)
            for s in range(2):
                part[s, own[s], :, :, j * 512 : (j + 1) * 512] = down[s]

    back = [{}, {}]
    near = (2, 1, 3, 0)

    def give_back(k):
        for i in near:
            for s in range(2):
                ii = (inner_at[s] + i) % SIDE
                back[s][k, i] = go([
                    remote(
                        part.at[s, (outer_at[s] + k) % SIDE, ii], in1.at[s, k - 1, i],
                        along[outer[s]](k),
                    )
                ])[0]

    def arrived(d):
        got([two[s][k][d] for k in (0, 1, 3, 2) for s in range(2)])

    feed(0)

    @pl.when(core == 0)
    def _():
        last_c.wait_recv()
        tell_final()

    arrived(1)
    feed(3)
    give_back(3)
    arrived(3)
    feed(1)
    give_back(1)
    arrived(2)
    feed(2)

    all_but_one(last_b, chips - 1, 4).wait_recv()
    unpack(last_b)
    done_with(load_voc)
    pick = (
        order[...] == lax.broadcasted_iota(jnp.int32, (ROWS, ROWS), 0)
    ).astype(BF16)
    final_rows = nn_dot(pick, last_x[...]).astype(BF16)
    top = None
    for start in range(0, VOC, VOC_BLOCK):
        stop = min(start + VOC_BLOCK, VOC)
        block = nt_dot(final_rows, voc[start:stop])
        logp[:, start:stop] = block
        m = jnp.max(block, axis=1, keepdims=True)
        top = m if top is None else jnp.maximum(top, m)
    total = jnp.sum(jnp.exp(logp[...] - top), axis=1, keepdims=True)
    eye = lax.broadcasted_iota(jnp.int32, (ROWS, ROWS), 0) == lax.broadcasted_iota(
        jnp.int32, (ROWS, ROWS), 1
    )

    def as_row(col):
        return jnp.sum(jnp.where(eye, col, 0.0), axis=0, keepdims=True)

    me = req * 2 + core
    stats[me] = jnp.concatenate([as_row(top), as_row(total)], axis=1)

    def tell(d, carry):
        q = lax.rem(me + d, 2 * chips)
        pltpu.make_async_remote_copy(
            src_ref=stats.at[me], dst_ref=stats.at[me], send_sem=gsem.at[6], recv_sem=gsem.at[7],
            device_id=(q // 2, q % 2), device_id_type=MESH,
        ).start()
        return carry

    lax.fori_loop(1, 2 * chips, tell, 0)
    give_back(2)

    ends = [{}, {}]
    keep = [None, None]
    for k in near:
        for s in range(2):
            got([back[s][o, k] for o in (3, 1, 2)])
            i = (inner_at[s] + k) % SIDE
            tot = part[s, outer_at[s], i].astype(F32)
            for d in range(3):
                tot += in1[s, d, k].astype(F32)
            if k == 0:
                keep[s] = tot
            else:
                mid[s, k - 1] = tot.astype(BF16)
                ends[s][k] = go([remote(mid.at[s, k - 1], in2.at[s, k - 1], along[inner[s]](k))])[0]
    for s in range(2):
        span = slice(s * PART, (s + 1) * PART)
        resid[span] = resid[span] + keep[s]

    all_but_one(stats, 2 * chips - 1, 6).wait_recv()
    tops = stats[:, 0, :ROWS]
    m = jnp.max(tops, axis=0, keepdims=True)
    t = jnp.sum(stats[:, 0, ROWS:] * jnp.exp(tops - m), axis=0, keepdims=True)
    top = jnp.sum(jnp.where(eye, m, 0.0), axis=1, keepdims=True)
    log_total = jnp.sum(jnp.where(eye, jnp.log(t), 0.0), axis=1, keepdims=True)
    logp[...] = logp[...] - top - log_total
    save_logp = local(logp, logp_hbm)
    save_logp.start()

    for s in range(2):
        got([ends[s][k] for k in (2, 1, 3)])
        span = slice(s * PART, (s + 1) * PART)
        tot = resid[span]
        for d in range(3):
            tot += in2[s, d].astype(F32)
        resid[span] = tot
    stay = pl.ds(pl.multiple_of(core * (D // 2), D // 2), D // 2)
    give = pl.ds(pl.multiple_of(other * (D // 2), D // 2), D // 2)
    out_s[...] = resid[:, give].astype(BF16)
    out_x = go([remote(out_s, out_r, sibling)])
    out[mine] = resid[:, stay].astype(BF16)

    @pl.when(core == 1)
    def _():
        all_but_one(last_a, chips - 1, 0).wait_send()
        all_but_one(last_p, chips - 1, 2).wait_send()

    all_but_one(last_b, chips - 1, 4).wait_send()
    all_but_one(stats, 2 * chips - 1, 6).wait_send()
    for c in sent[:-1]:
        c.wait_send()
    got(out_x)
    out[theirs] = out_r[...]
    save_out = local(out, out_hbm)
    save_out.start()
    out_x[0].wait_send()
    save_logp.wait()
    save_out.wait()


def on_device(
    hidden_in, attn_gain, w_query, w_key, w_value, query_gain, key_gain, w_out,
    cache_keys, cache_values, cache_lengths, slot_request, mlp_gain, w_gate, w_up, w_down,
    final_gain, w_vocab,
):
    half_dim = HEAD_DIM // 2
    one = ROPE_BASE ** (-2.0 * np.arange(half_dim) / HEAD_DIM)
    freq = jnp.asarray(np.concatenate([one, one])[None].astype(np.float32))
    vmem = pl.BlockSpec(memory_space=pltpu.VMEM)
    smem = pl.BlockSpec(memory_space=pltpu.SMEM)
    far = pl.BlockSpec(memory_space=pl.ANY)
    V = pltpu.VMEM
    S = SIDE
    results = (
        jax.ShapeDtypeStruct((ROWS, D // 2), BF16),
        jax.ShapeDtypeStruct((ROWS, VOC), F32),
    )
    out, logp = pl.pallas_call(
        step_kernel,
        out_shape=results,
        in_specs=[vmem] * 8 + [smem] * 2 + [far] * 10,
        out_specs=(far, far),
        scratch_shapes=[
            V((ROWS, D // 2), BF16), V((ROWS, VOC), F32),
            V((ROWS, D), BF16),
            V((D, 1024), BF16), V((D, 512), BF16), V((D, 512), BF16), V((1024, D), BF16),
            V((KEYS, 512), BF16), V((KEYS, 512), BF16), V((VOC, D), BF16),
            V((2, 3, PLANE_UNITS, D // 2), BF16),
            V((4, 2 * ROWS, HEAD_DIM), BF16), V((4, ROWS, HEAD_DIM), BF16), V((ROWS, 512), BF16),
            V((ROWS, 1024), BF16), V((ROWS, D), F32), V((HALF, D), F32), V((16, 128), F32),
            V((HALF, D), F32),
            V((2, S, S, PART, D), BF16), V((2, S, S, PART, D), BF16),
            V((2, 3, S, PART, D), BF16), V((2, 3, PART, D), BF16), V((2, 3, PART, D), BF16),
            V((HALF, D // 2), BF16), V((HALF, D // 2), BF16),
            V((S**3, 16, 128), BF16), V((S**3, 16, 128), BF16), V((S**3, 16, 128), BF16),
            V((S**3, 16, 128), BF16), V((16, 128), F32), V((S**3 * 16, 128), F32),
            V((S**3, D), BF16), V((2 * S**3, 1, 128), F32),
            pltpu.SemaphoreType.DMA((32,)),
            pltpu.SemaphoreType.DMA((N_COPIES,)),
            pltpu.SemaphoreType.DMA((N_COPIES,)),
            pltpu.SemaphoreType.DMA((8,)),
            pltpu.SemaphoreType.REGULAR,
            pltpu.SemaphoreType.REGULAR,
        ],
        compiler_params=pltpu.CompilerParams(
            collective_id=0, has_side_effects=True, vmem_limit_bytes=58 * 1024 * 1024
        ),
    )(
        hidden_in, attn_gain.reshape(1, D), query_gain.reshape(1, HEAD_DIM),
        key_gain.reshape(1, HEAD_DIM), mlp_gain.reshape(8, 128), final_gain.reshape(16, 128), freq,
        slot_request.reshape(1, ROWS), slot_request, cache_lengths,
        w_query, w_key, w_value, w_out, cache_keys, cache_values,
        w_gate.T, w_up.T, w_down, w_vocab.T,
    )
    return out, logp


def solution(mesh):
    in_specs = (
        P("req", None), P(), P(None, "head"), P(None, "head"), P(None, "head"), P(), P(),
        P("head", None), P("req", None, "head"), P("req", None, "head"), P(), P(), P("head"),
        P("head", "req"), P("head", "req"), P("req", "head"), P(), P(None, ("req", "head")),
    )
    out_specs = (P("req", "head"), P(None, ("req", "head")))
    return jax.shard_map(
        on_device, mesh=mesh, in_specs=in_specs, out_specs=out_specs, check_vma=False
    )
```

```python
import functools
import math

import jax
import jax.numpy as jnp
import numpy as np
from jax import lax
from jax.experimental import pallas as pl
from jax.experimental.pallas import tpu as pltpu
from jax.sharding import PartitionSpec as P

MESH = pl.DeviceIdType.MESH
F32, BF16 = jnp.float32, jnp.bfloat16

D = 2048
HEAD_DIM = 128
ROPE_BASE = 1000000.0
EPS = 1e-06
SHIFT = 4.0
LOG2E = math.log2(math.e)

SIDE = 4
ROWS = 64
HALF = ROWS // 2
PART = HALF // 2
UNITS = 96
PLANE_UNITS = SIDE * UNITS
KEYS = 2048
KEY_BLOCK = 1024
VOC = 1187
VOC_BLOCK = 256
N_COPIES = 100


def nt_dot(a, b):
    return lax.dot_general(a, b, (((1,), (1,)), ((), ())), preferred_element_type=F32)


def nn_dot(a, b):
    return jnp.dot(a, b, preferred_element_type=F32)


def step_kernel(
    hidden, attn_gain, query_gain, key_gain, mlp_gain, final_gain, freq, order, order_s, lengths,
    w_query, w_key, w_value, w_out, cache_k, cache_v, w_gate, w_up, w_down, w_vocab,
    out_hbm, logp_hbm,
    out, logp, normed, wq, wk, wv, wo, kc, vc, voc, wf, qs, kn, vn, att, proj, proj_in, gains, resid,
    rows, part, in1, mid, in2, out_s, out_r,
    last_a, last_p, last_in, last_b, last_res, spread, last_x, stats,
    lsem, ssem, rsem, gsem, plane_sem, all_sem,
):
    req = lax.axis_index("req")
    core = lax.axis_index("head")
    other = 1 - core
    y = req // (SIDE * SIDE)
    x = (req // SIDE) % SIDE
    z = req % SIDE

    def at(yy, xx, zz, cc):
        return ((yy % SIDE) * (SIDE * SIDE) + (xx % SIDE) * SIDE + (zz % SIDE), cc)

    along = {
        "y": lambda d: at(y + d, x, z, core),
        "x": lambda d: at(y, x + d, z, core),
        "z": lambda d: at(y, x, z + d, core),
    }
    sibling = (req, other)
    counters = {"local": 0, "remote": 0}

    def local(src, dst):
        i = counters["local"]
        counters["local"] = i + 1
        return pltpu.make_async_copy(src, dst, lsem.at[i])

    def remote(src, dst, device):
        i = counters["remote"]
        counters["remote"] = i + 1
        return pltpu.make_async_remote_copy(
            src_ref=src, dst_ref=dst, send_sem=ssem.at[i], recv_sem=rsem.at[i],
            device_id=device, device_id_type=MESH,
        )

    sent = []

    def go(copies):
        for c in copies:
            c.start()
            sent.append(c)
        return copies

    def got(copies):
        for c in copies:
            c.wait_recv()

    def load(src, dst, parts):
        n = src.shape[0] // parts
        return [local(src.at[pl.ds(k * n, n)], dst.at[pl.ds(k * n, n)]) for k in range(parts)]

    def begin(copies):
        for c in copies:
            c.start()

    def done_with(copies):
        for c in copies:
            c.wait()

    load_k = load(w_key, wk, 2)
    load_v = load(w_value, wv, 2)
    load_q = load(w_query, wq, 4)
    load_kc = load(cache_k.at[0], kc, 2)
    load_vc = load(cache_v.at[0], vc, 2)
    load_o = load(w_out, wo, 4)
    load_voc = [local(w_vocab, voc)]
    unit_at = pl.multiple_of(z * UNITS, UNITS)
    load_own = [
        local(w, wf.at[core, k, pl.ds(unit_at, UNITS)]) for k, w in enumerate((w_gate, w_up, w_down))
    ]
    my_gain = gains.at[pl.ds(pl.multiple_of(core * 8, 8), 8)]
    load_gain = local(mlp_gain, my_gain)
    begin(load_own + [load_gain] + load_k + load_v + load_q + load_kc + load_vc + load_o)

    barrier = pltpu.get_barrier_semaphore()
    peers = [sibling]
    for d in (1, 2, 3):
        peers += [along["x"](d), at(y, x + d, z, other), along["y"](d), along["z"](d)]
    for p in peers:
        pl.semaphore_signal(barrier, inc=1, device_id=p, device_id_type=MESH)

    def shard(zz, h):
        return wf.at[h, :, pl.ds(pl.multiple_of(zz * UNITS, UNITS), UNITS)]

    def half_shard(zz, h, k):
        n = UNITS // 2
        return wf.at[h, :, pl.ds(pl.multiple_of(zz * UNITS + k * n, n), n)]

    zm, zp, zo = (z + 3) % SIDE, (z + 1) % SIDE, (z + 2) % SIDE
    done_with(load_own + [load_gain])
    pl.semaphore_wait(barrier, len(peers))
    w_first, w_second = [], []
    for copies, k_up in ((w_first, 0), (w_second, 1)):
        copies += go([
            remote(half_shard(z, core, k_up), half_shard(z, core, k_up), along["z"](1)),
            remote(half_shard(z, core, 1 - k_up), half_shard(z, core, 1 - k_up), along["z"](-1)),
        ])
    gain_x = go([remote(my_gain, my_gain, sibling)])
    w_sib = go([remote(shard(z, core), shard(z, core), sibling)])
    for d in (1, 2, 3):
        pl.semaphore_signal(plane_sem, inc=1, device_id=along["y"](d), device_id_type=MESH)

    tokens = hidden[...].astype(F32)
    scale = lax.rsqrt(jnp.mean(tokens * tokens, axis=-1, keepdims=True) + EPS)
    normed[...] = (tokens * scale * attn_gain[...]).astype(BF16)
    slot = order_s[req]
    length = lengths[slot]
    position = (length + lax.broadcasted_iota(jnp.int32, (ROWS, 1), 0)).astype(F32)
    angle = position * freq[...]
    cosine = jnp.cos(angle)
    lane = lax.broadcasted_iota(jnp.int32, (ROWS, HEAD_DIM), 1)
    sine = jnp.where(lane < HEAD_DIM // 2, -jnp.sin(angle), jnp.sin(angle))

    def rotated(v, gain):
        v = v * lax.rsqrt(jnp.mean(v * v, axis=-1, keepdims=True) + EPS) * gain
        return (v * cosine + pltpu.roll(v, HEAD_DIM // 2, 1) * sine).astype(BF16)

    done_with(load_k)
    for j in range(2):
        both = nn_dot(normed[...], wk[:, j * 256 : (j + 1) * 256])
        for i in range(2):
            kn[2 * j + i] = rotated(both[:, i * 128 : (i + 1) * 128], key_gain[...])
    done_with(load_v)
    for j in range(2):
        vn[:, j * 256 : (j + 1) * 256] = nn_dot(
            normed[...], wv[:, j * 256 : (j + 1) * 256]
        ).astype(BF16)

    done_with(load_q)
    for j in range(4):
        both = nn_dot(normed[...], wq[:, j * 256 : (j + 1) * 256])
        for i in range(2):
            qs[j, i * ROWS : (i + 1) * ROWS] = rotated(
                both[:, i * 128 : (i + 1) * 128], query_gain[...]
            )

    done_with(load_kc)
    done_with(load_vc)
    begin(load_voc)
    slope = LOG2E / math.sqrt(HEAD_DIM)
    base = SHIFT * LOG2E
    row_at = lax.broadcasted_iota(jnp.int32, (2 * ROWS, ROWS), 0) % ROWS
    causal = row_at >= lax.broadcasted_iota(jnp.int32, (2 * ROWS, ROWS), 1)

    def one_head(g):
        q = qs[g]
        cols = slice(g * HEAD_DIM, (g + 1) * HEAD_DIM)
        fresh = jnp.where(causal, jnp.exp2(nt_dot(q, kn[g]) * slope - base), 0.0)
        total = jnp.sum(fresh, axis=1, keepdims=True)
        acc = nn_dot(fresh.astype(BF16), vn[:, cols])
        for b in range(KEYS // KEY_BLOCK):
            span = slice(b * KEY_BLOCK, (b + 1) * KEY_BLOCK)
            s = nt_dot(q, kc[span, cols])
            key_at = b * KEY_BLOCK + lax.broadcasted_iota(jnp.int32, s.shape, 1)
            p = jnp.where(key_at < length, jnp.exp2(s * slope - base), 0.0)
            total = total + jnp.sum(p, axis=1, keepdims=True)
            acc = acc + nn_dot(p.astype(BF16), vc[span, cols])
        done = (acc / total).astype(BF16)
        att[:, 2 * g * HEAD_DIM : (2 * g + 1) * HEAD_DIM] = done[:ROWS]
        att[:, (2 * g + 1) * HEAD_DIM : (2 * g + 2) * HEAD_DIM] = done[ROWS:]

    for g in range(4):
        one_head(g)

    done_with(load_o)
    for j in range(4):
        cols = slice(j * 512, (j + 1) * 512)
        proj[:, cols] = nn_dot(att[...], wo[:, cols])
    mine = pl.ds(pl.multiple_of(core * HALF, HALF), HALF)
    theirs = pl.ds(pl.multiple_of(other * HALF, HALF), HALF)
    proj_x = go([remote(proj.at[theirs], proj_in, sibling)])
    pl.semaphore_wait(plane_sem, 3)
    for d in (1, 2, 3):
        pl.semaphore_signal(all_sem, inc=1, device_id=along["z"](d), device_id_type=MESH)
    got(gain_x + proj_x)
    r = hidden[mine].astype(F32) + (proj[mine] + proj_in[...])
    resid[...] = r
    scale = lax.rsqrt(jnp.mean(r * r, axis=-1, keepdims=True) + EPS)
    for j in range(D // 128):
        cols = slice(j * 128, (j + 1) * 128)
        mixed = (r[:, cols] * scale * gains[j : j + 1]).astype(BF16)
        rows[0, y, x, :, cols] = mixed[:PART]
        rows[1, x, y, :, cols] = mixed[PART:]

    inner, outer = ("x", "y"), ("y", "x")
    inner_at, outer_at = (x, y), (y, x)
    hops = (1, 3, 2)

    def piece(s, o, i):
        return rows.at[s, o % SIDE, i % SIDE]

    def push(s, i, axis):
        b = piece(s, outer_at[s], i)
        return {d: go([remote(b, b, along[axis](d))])[0] for d in hops}

    def each_chip(body):
        def step(d, carry):
            body(lax.rem(req + d, SIDE * SIDE * SIDE))
            return carry

        lax.fori_loop(1, SIDE**3, step, 0)

    def all_but_one(buf, n, k):
        return pltpu.make_async_remote_copy(
            src_ref=buf.at[pl.ds(0, n)], dst_ref=buf.at[pl.ds(0, n)],
            send_sem=gsem.at[k], recv_sem=gsem.at[k + 1], device_id=sibling, device_id_type=MESH,
        )

    def to_chip(src, dst, q, k):
        pltpu.make_async_remote_copy(
            src_ref=src, dst_ref=dst, send_sem=gsem.at[k], recv_sem=gsem.at[k + 1],
            device_id=(q, core), device_id_type=MESH,
        ).start()

    pl.semaphore_wait(all_sem, 3)
    chips = SIDE**3

    @pl.when(core == 1)
    def _():
        tile = jnp.concatenate(
            [resid[HALF - 1 : HALF, j * 128 : (j + 1) * 128] for j in range(16)], axis=0
        )
        last_res[...] = tile
        power = jnp.sum(jnp.sum(tile * tile, axis=1, keepdims=True), axis=0, keepdims=True)
        last_a[req] = (tile * lax.rsqrt(power / D + EPS) * gains[...]).astype(BF16)
        each_chip(lambda q: to_chip(last_a.at[req], last_a.at[req], q, 0))

    one = [push(s, inner_at[s], inner[s]) for s in range(2)]
    two = [{0: push(s, inner_at[s], outer[s])} for s in range(2)]
    got(w_first)
    w_on = go([
        remote(half_shard(zm, core, 0), half_shard(zm, core, 0), along["z"](1)),
        remote(half_shard(zp, core, 1), half_shard(zp, core, 1), along["z"](-1)),
    ])

    def unpack(tiles):
        spread[...] = tiles[...].astype(F32).reshape(chips * 16, 128)
        for j in range(16):
            last_x[:, j * 128 : (j + 1) * 128] = spread[pl.ds(j, chips, stride=16)].astype(BF16)

    got(w_sib[:1])

    @pl.when(core == 1)
    def _():
        all_but_one(last_a, chips - 1, 0).wait_recv()
        unpack(last_a)
        units = pl.ds(unit_at, UNITS)
        lo, hi = last_x[:, : D // 2], last_x[:, D // 2 :]
        gate = nt_dot(lo, wf[0, 0, units]) + nt_dot(hi, wf[1, 0, units])
        up = nt_dot(lo, wf[0, 1, units]) + nt_dot(hi, wf[1, 1, units])
        active = (gate / (1.0 + jnp.exp(-gate)) * up).astype(BF16)
        for h in range(2):
            down = nn_dot(active, wf[h, 2, units])
            for j in range(8):
                spread[pl.ds(8 * h + j, chips, stride=16)] = down[:, j * 128 : (j + 1) * 128]
        last_p[...] = spread[...].reshape(chips, 16, 128).astype(BF16)
        last_in[req] = last_p[req]
        each_chip(lambda q: to_chip(last_p.at[q], last_in.at[req], q, 2))

    for d in (1, 3, 2):
        for s in range(2):
            one[s][d].wait_recv()
            two[s][d] = push(s, inner_at[s] - d + SIDE, outer[s])

    got(w_second)
    w_sib += go([remote(shard(zm, core), shard(zm, core), sibling)])
    w_sib += go([remote(shard(zp, core), shard(zp, core), sibling)])
    got(w_on)
    w_sib += go([remote(shard(zo, core), shard(zo, core), sibling)])

    last_c = remote(last_b.at[req], last_b.at[req], sibling)

    def tell_final():
        each_chip(lambda q: to_chip(last_b.at[req], last_b.at[req], q, 4))

    @pl.when(core == 1)
    def _():
        all_but_one(last_in, chips - 1, 2).wait_recv()
        tile = last_res[...] + jnp.sum(last_in[...].astype(F32), axis=0)
        power = jnp.sum(jnp.sum(tile * tile, axis=1, keepdims=True), axis=0, keepdims=True)
        last_b[req] = (tile * lax.rsqrt(power / D + EPS) * final_gain[...]).astype(BF16)
        last_c.start()
        tell_final()
        last_c.wait_send()

    got(w_sib[1:])
    block_rows = SIDE * PART

    def feed(k):
        own = [(outer_at[s] + k) % SIDE for s in range(2)]
        xa = jnp.concatenate([rows[s, own[s]].reshape(block_rows, D) for s in range(2)], axis=0)
        gu = nt_dot(xa[:, : D // 2], wf[0, 0:2].reshape(2 * PLANE_UNITS, D // 2))
        gu += nt_dot(xa[:, D // 2 :], wf[1, 0:2].reshape(2 * PLANE_UNITS, D // 2))
        gate, up = gu[:, :PLANE_UNITS], gu[:, PLANE_UNITS:]
        active = (gate / (1.0 + jnp.exp(-gate)) * up).astype(BF16)
        for j in range(4):
            down = nn_dot(active, wf[j // 2, 2, :, (j % 2) * 512 : (j % 2 + 1) * 512])
            down = down.astype(BF16).reshape(2, SIDE, PART, 512)
            for s in range(2):
                part[s, own[s], :, :, j * 512 : (j + 1) * 512] = down[s]

    back = [{}, {}]
    near = (2, 1, 3, 0)

    def give_back(k):
        for i in near:
            for s in range(2):
                ii = (inner_at[s] + i) % SIDE
                back[s][k, i] = go([
                    remote(
                        part.at[s, (outer_at[s] + k) % SIDE, ii], in1.at[s, k - 1, i],
                        along[outer[s]](k),
                    )
                ])[0]

    def arrived(d):
        got([two[s][k][d] for k in (0, 1, 3, 2) for s in range(2)])

    arrived(1)
    feed(3)

    @pl.when(core == 0)
    def _():
        last_c.wait_recv()
        tell_final()

    give_back(3)
    arrived(3)
    feed(1)
    give_back(1)
    arrived(2)
    feed(2)
    give_back(2)
    feed(0)

    all_but_one(last_b, chips - 1, 4).wait_recv()
    unpack(last_b)
    done_with(load_voc)
    pick = (
        order[...] == lax.broadcasted_iota(jnp.int32, (ROWS, ROWS), 0)
    ).astype(BF16)
    final_rows = nn_dot(pick, last_x[...]).astype(BF16)
    top = None
    for start in range(0, VOC, VOC_BLOCK):
        stop = min(start + VOC_BLOCK, VOC)
        block = nt_dot(final_rows, voc[start:stop])
        logp[:, start:stop] = block
        m = jnp.max(block, axis=1, keepdims=True)
        top = m if top is None else jnp.maximum(top, m)
    total = jnp.sum(jnp.exp(logp[...] - top), axis=1, keepdims=True)
    eye = lax.broadcasted_iota(jnp.int32, (ROWS, ROWS), 0) == lax.broadcasted_iota(
        jnp.int32, (ROWS, ROWS), 1
    )

    def as_row(col):
        return jnp.sum(jnp.where(eye, col, 0.0), axis=0, keepdims=True)

    me = req * 2 + core
    stats[me] = jnp.concatenate([as_row(top), as_row(total)], axis=1)

    def tell(d, carry):
        q = lax.rem(me + d, 2 * chips)
        pltpu.make_async_remote_copy(
            src_ref=stats.at[me], dst_ref=stats.at[me], send_sem=gsem.at[6], recv_sem=gsem.at[7],
            device_id=(q // 2, q % 2), device_id_type=MESH,
        ).start()
        return carry

    lax.fori_loop(1, 2 * chips, tell, 0)

    ends = [{}, {}]
    keep = [None, None]
    for k in near:
        for s in range(2):
            got([back[s][o, k] for o in (3, 1, 2)])
            i = (inner_at[s] + k) % SIDE
            tot = part[s, outer_at[s], i].astype(F32)
            for d in range(3):
                tot += in1[s, d, k].astype(F32)
            if k == 0:
                keep[s] = tot
            else:
                mid[s, k - 1] = tot.astype(BF16)
                ends[s][k] = go([remote(mid.at[s, k - 1], in2.at[s, k - 1], along[inner[s]](k))])[0]
    for s in range(2):
        span = slice(s * PART, (s + 1) * PART)
        resid[span] = resid[span] + keep[s]

    all_but_one(stats, 2 * chips - 1, 6).wait_recv()
    tops = stats[:, 0, :ROWS]
    m = jnp.max(tops, axis=0, keepdims=True)
    t = jnp.sum(stats[:, 0, ROWS:] * jnp.exp(tops - m), axis=0, keepdims=True)
    top = jnp.sum(jnp.where(eye, m, 0.0), axis=1, keepdims=True)
    log_total = jnp.sum(jnp.where(eye, jnp.log(t), 0.0), axis=1, keepdims=True)
    logp[...] = logp[...] - top - log_total
    save_logp = local(logp, logp_hbm)
    save_logp.start()

    for s in range(2):
        got([ends[s][k] for k in (2, 1, 3)])
        span = slice(s * PART, (s + 1) * PART)
        tot = resid[span]
        for d in range(3):
            tot += in2[s, d].astype(F32)
        resid[span] = tot
    stay = pl.ds(pl.multiple_of(core * (D // 2), D // 2), D // 2)
    give = pl.ds(pl.multiple_of(other * (D // 2), D // 2), D // 2)
    out_s[...] = resid[:, give].astype(BF16)
    out_x = go([remote(out_s, out_r, sibling)])
    out[mine] = resid[:, stay].astype(BF16)

    @pl.when(core == 1)
    def _():
        all_but_one(last_a, chips - 1, 0).wait_send()
        all_but_one(last_p, chips - 1, 2).wait_send()

    all_but_one(last_b, chips - 1, 4).wait_send()
    all_but_one(stats, 2 * chips - 1, 6).wait_send()
    for c in sent[:-1]:
        c.wait_send()
    got(out_x)
    out[theirs] = out_r[...]
    save_out = local(out, out_hbm)
    save_out.start()
    out_x[0].wait_send()
    save_logp.wait()
    save_out.wait()


def copy_kernel(a, b, a_out, b_out):
    a_out[...] = a[...]
    b_out[...] = b[...]


def on_device(
    hidden_in, attn_gain, w_query, w_key, w_value, query_gain, key_gain, w_out,
    cache_keys, cache_values, cache_lengths, slot_request, mlp_gain, w_gate, w_up, w_down,
    final_gain, w_vocab,
):
    half_dim = HEAD_DIM // 2
    one = ROPE_BASE ** (-2.0 * np.arange(half_dim) / HEAD_DIM)
    freq = jnp.asarray(np.concatenate([one, one])[None].astype(np.float32))
    vmem = pl.BlockSpec(memory_space=pltpu.VMEM)
    smem = pl.BlockSpec(memory_space=pltpu.SMEM)
    far = pl.BlockSpec(memory_space=pl.ANY)
    V = pltpu.VMEM
    S = SIDE
    results = (
        jax.ShapeDtypeStruct((ROWS, D // 2), BF16),
        jax.ShapeDtypeStruct((ROWS, VOC), F32),
    )
    out, logp = pl.pallas_call(
        step_kernel,
        out_shape=results,
        in_specs=[vmem] * 8 + [smem] * 2 + [far] * 10,
        out_specs=(far, far),
        scratch_shapes=[
            V((ROWS, D // 2), BF16), V((ROWS, VOC), F32),
            V((ROWS, D), BF16),
            V((D, 1024), BF16), V((D, 512), BF16), V((D, 512), BF16), V((1024, D), BF16),
            V((KEYS, 512), BF16), V((KEYS, 512), BF16), V((VOC, D), BF16),
            V((2, 3, PLANE_UNITS, D // 2), BF16),
            V((4, 2 * ROWS, HEAD_DIM), BF16), V((4, ROWS, HEAD_DIM), BF16), V((ROWS, 512), BF16),
            V((ROWS, 1024), BF16), V((ROWS, D), F32), V((HALF, D), F32), V((16, 128), F32),
            V((HALF, D), F32),
            V((2, S, S, PART, D), BF16), V((2, S, S, PART, D), BF16),
            V((2, 3, S, PART, D), BF16), V((2, 3, PART, D), BF16), V((2, 3, PART, D), BF16),
            V((HALF, D // 2), BF16), V((HALF, D // 2), BF16),
            V((S**3, 16, 128), BF16), V((S**3, 16, 128), BF16), V((S**3, 16, 128), BF16),
            V((S**3, 16, 128), BF16), V((16, 128), F32), V((S**3 * 16, 128), F32),
            V((S**3, D), BF16), V((2 * S**3, 1, 128), F32),
            pltpu.SemaphoreType.DMA((32,)),
            pltpu.SemaphoreType.DMA((N_COPIES,)),
            pltpu.SemaphoreType.DMA((N_COPIES,)),
            pltpu.SemaphoreType.DMA((8,)),
            pltpu.SemaphoreType.REGULAR,
            pltpu.SemaphoreType.REGULAR,
        ],
        compiler_params=pltpu.CompilerParams(
            collective_id=0, has_side_effects=True, vmem_limit_bytes=58 * 1024 * 1024
        ),
    )(
        hidden_in, attn_gain.reshape(1, D), query_gain.reshape(1, HEAD_DIM),
        key_gain.reshape(1, HEAD_DIM), mlp_gain.reshape(8, 128), final_gain.reshape(16, 128), freq,
        slot_request.reshape(1, ROWS), slot_request, cache_lengths,
        w_query, w_key, w_value, w_out, cache_keys, cache_values,
        w_gate.T, w_up.T, w_down, w_vocab.T,
    )
    return pl.pallas_call(
        copy_kernel,
        out_shape=results,
        in_specs=[vmem] * 2,
        out_specs=(vmem, vmem),
    )(out, logp)


def solution(mesh):
    in_specs = (
        P("req", None), P(), P(None, "head"), P(None, "head"), P(None, "head"), P(), P(),
        P("head", None), P("req", None, "head"), P("req", None, "head"), P(), P(), P("head"),
        P("head", "req"), P("head", "req"), P("req", "head"), P(), P(None, ("req", "head")),
    )
    out_specs = (P("req", "head"), P(None, ("req", "head")))
    return jax.shard_map(
        on_device, mesh=mesh, in_specs=in_specs, out_specs=out_specs, check_vma=False
    )
```

```python
import functools
import math

import jax
import jax.numpy as jnp
import numpy as np
from jax import lax
from jax.experimental import pallas as pl
from jax.experimental.pallas import tpu as pltpu
from jax.sharding import PartitionSpec as P

MESH = pl.DeviceIdType.MESH
F32, BF16 = jnp.float32, jnp.bfloat16

D = 2048
HEAD_DIM = 128
ROPE_BASE = 1000000.0
EPS = 1e-06
SHIFT = 4.0
LOG2E = math.log2(math.e)

SIDE = 4
ROWS = 64
HALF = ROWS // 2
PART = HALF // 2
UNITS = 96
PLANE_UNITS = SIDE * UNITS
KEYS = 2048
KEY_BLOCK = 1024
VOC = 1187
VOC_BLOCK = 256
N_COPIES = 100


def nt_dot(a, b):
    return lax.dot_general(a, b, (((1,), (1,)), ((), ())), preferred_element_type=F32)


def nn_dot(a, b):
    return jnp.dot(a, b, preferred_element_type=F32)


def step_kernel(
    hidden, attn_gain, query_gain, key_gain, mlp_gain, final_gain, freq, order, order_s, lengths,
    w_query, w_key, w_value, w_out, cache_k, cache_v, w_gate, w_up, w_down, w_vocab,
    out_hbm, logp_hbm,
    out, logp, normed, wq, wk, wv, wo, kc, vc, voc, wf, qs, kn, vn, att, proj, proj_in, gains, resid,
    rows, part, in1, mid, in2, out_s, out_r,
    last_a, last_p, last_in, last_b, last_res, spread, last_x, stats,
    lsem, ssem, rsem, gsem, plane_sem, all_sem,
):
    req = lax.axis_index("req")
    core = lax.axis_index("head")
    other = 1 - core
    y = req // (SIDE * SIDE)
    x = (req // SIDE) % SIDE
    z = req % SIDE

    def at(yy, xx, zz, cc):
        return ((yy % SIDE) * (SIDE * SIDE) + (xx % SIDE) * SIDE + (zz % SIDE), cc)

    along = {
        "y": lambda d: at(y + d, x, z, core),
        "x": lambda d: at(y, x + d, z, core),
        "z": lambda d: at(y, x, z + d, core),
    }
    sibling = (req, other)
    counters = {"local": 0, "remote": 0}

    def local(src, dst):
        i = counters["local"]
        counters["local"] = i + 1
        return pltpu.make_async_copy(src, dst, lsem.at[i])

    def remote(src, dst, device):
        i = counters["remote"]
        counters["remote"] = i + 1
        return pltpu.make_async_remote_copy(
            src_ref=src, dst_ref=dst, send_sem=ssem.at[i], recv_sem=rsem.at[i],
            device_id=device, device_id_type=MESH,
        )

    sent = []

    def go(copies):
        for c in copies:
            c.start()
            sent.append(c)
        return copies

    def got(copies):
        for c in copies:
            c.wait_recv()

    def load(src, dst, parts):
        n = src.shape[0] // parts
        return [local(src.at[pl.ds(k * n, n)], dst.at[pl.ds(k * n, n)]) for k in range(parts)]

    def begin(copies):
        for c in copies:
            c.start()

    def done_with(copies):
        for c in copies:
            c.wait()

    load_k = load(w_key, wk, 2)
    load_v = load(w_value, wv, 2)
    load_q = load(w_query, wq, 4)
    load_kc = load(cache_k.at[0], kc, 2)
    load_vc = load(cache_v.at[0], vc, 2)
    load_o = load(w_out, wo, 4)
    load_voc = [local(w_vocab, voc)]
    unit_at = pl.multiple_of(z * UNITS, UNITS)
    load_own = [
        local(w, wf.at[core, k, pl.ds(unit_at, UNITS)]) for k, w in enumerate((w_gate, w_up, w_down))
    ]
    my_gain = gains.at[pl.ds(pl.multiple_of(core * 8, 8), 8)]
    load_gain = local(mlp_gain, my_gain)
    begin(load_own + [load_gain] + load_k + load_v + load_q + load_kc + load_vc + load_o)

    barrier = pltpu.get_barrier_semaphore()
    peers = [sibling]
    for d in (1, 2, 3):
        peers += [along["x"](d), at(y, x + d, z, other), along["y"](d), along["z"](d)]
    for p in peers:
        pl.semaphore_signal(barrier, inc=1, device_id=p, device_id_type=MESH)

    def shard(zz, h):
        return wf.at[h, :, pl.ds(pl.multiple_of(zz * UNITS, UNITS), UNITS)]

    def half_shard(zz, h, k):
        n = UNITS // 2
        return wf.at[h, :, pl.ds(pl.multiple_of(zz * UNITS + k * n, n), n)]

    zm, zp, zo = (z + 3) % SIDE, (z + 1) % SIDE, (z + 2) % SIDE
    done_with(load_own + [load_gain])
    pl.semaphore_wait(barrier, len(peers))
    w_first, w_second = [], []
    for copies, k_up in ((w_first, 0), (w_second, 1)):
        copies += go([
            remote(half_shard(z, core, k_up), half_shard(z, core, k_up), along["z"](1)),
            remote(half_shard(z, core, 1 - k_up), half_shard(z, core, 1 - k_up), along["z"](-1)),
        ])
    gain_x = go([remote(my_gain, my_gain, sibling)])
    w_sib = go([remote(shard(z, core), shard(z, core), sibling)])
    for d in (1, 2, 3):
        pl.semaphore_signal(plane_sem, inc=1, device_id=along["y"](d), device_id_type=MESH)

    tokens = hidden[...].astype(F32)
    scale = lax.rsqrt(jnp.mean(tokens * tokens, axis=-1, keepdims=True) + EPS)
    normed[...] = (tokens * scale * attn_gain[...]).astype(BF16)
    slot = order_s[req]
    length = lengths[slot]
    position = (length + lax.broadcasted_iota(jnp.int32, (ROWS, 1), 0)).astype(F32)
    angle = position * freq[...]
    cosine = jnp.cos(angle)
    lane = lax.broadcasted_iota(jnp.int32, (ROWS, HEAD_DIM), 1)
    sine = jnp.where(lane < HEAD_DIM // 2, -jnp.sin(angle), jnp.sin(angle))

    def rotated(v, gain):
        v = v * lax.rsqrt(jnp.mean(v * v, axis=-1, keepdims=True) + EPS) * gain
        return (v * cosine + pltpu.roll(v, HEAD_DIM // 2, 1) * sine).astype(BF16)

    done_with(load_k)
    for j in range(2):
        both = nn_dot(normed[...], wk[:, j * 256 : (j + 1) * 256])
        for i in range(2):
            kn[2 * j + i] = rotated(both[:, i * 128 : (i + 1) * 128], key_gain[...])
    done_with(load_v)
    for j in range(2):
        vn[:, j * 256 : (j + 1) * 256] = nn_dot(
            normed[...], wv[:, j * 256 : (j + 1) * 256]
        ).astype(BF16)

    done_with(load_q)
    for j in range(4):
        both = nn_dot(normed[...], wq[:, j * 256 : (j + 1) * 256])
        for i in range(2):
            qs[j, i * ROWS : (i + 1) * ROWS] = rotated(
                both[:, i * 128 : (i + 1) * 128], query_gain[...]
            )

    done_with(load_kc)
    done_with(load_vc)
    begin(load_voc)
    slope = LOG2E / math.sqrt(HEAD_DIM)
    base = SHIFT * LOG2E
    row_at = lax.broadcasted_iota(jnp.int32, (2 * ROWS, ROWS), 0) % ROWS
    causal = row_at >= lax.broadcasted_iota(jnp.int32, (2 * ROWS, ROWS), 1)

    def one_head(g):
        q = qs[g]
        cols = slice(g * HEAD_DIM, (g + 1) * HEAD_DIM)
        fresh = jnp.where(causal, jnp.exp2(nt_dot(q, kn[g]) * slope - base), 0.0)
        total = jnp.sum(fresh, axis=1, keepdims=True)
        acc = nn_dot(fresh.astype(BF16), vn[:, cols])
        for b in range(KEYS // KEY_BLOCK):
            span = slice(b * KEY_BLOCK, (b + 1) * KEY_BLOCK)
            s = nt_dot(q, kc[span, cols])
            key_at = b * KEY_BLOCK + lax.broadcasted_iota(jnp.int32, s.shape, 1)
            p = jnp.where(key_at < length, jnp.exp2(s * slope - base), 0.0)
            total = total + jnp.sum(p, axis=1, keepdims=True)
            acc = acc + nn_dot(p.astype(BF16), vc[span, cols])
        done = (acc / total).astype(BF16)
        att[:, 2 * g * HEAD_DIM : (2 * g + 1) * HEAD_DIM] = done[:ROWS]
        att[:, (2 * g + 1) * HEAD_DIM : (2 * g + 2) * HEAD_DIM] = done[ROWS:]

    for g in range(4):
        one_head(g)

    done_with(load_o)
    mine = pl.ds(pl.multiple_of(core * HALF, HALF), HALF)
    theirs = pl.ds(pl.multiple_of(other * HALF, HALF), HALF)
    proj_x = []
    for j in range(4):
        cols = slice(j * 512, (j + 1) * 512)
        proj[:, cols] = nn_dot(att[...], wo[:, cols])
        proj_x += go([
            remote(proj.at[theirs, pl.ds(j * 512, 512)], proj_in.at[:, pl.ds(j * 512, 512)], sibling)
        ])
    pl.semaphore_wait(plane_sem, 3)
    for d in (1, 2, 3):
        pl.semaphore_signal(all_sem, inc=1, device_id=along["z"](d), device_id_type=MESH)
    got(gain_x + proj_x)
    r = hidden[mine].astype(F32) + (proj[mine] + proj_in[...])
    resid[...] = r
    scale = lax.rsqrt(jnp.mean(r * r, axis=-1, keepdims=True) + EPS)
    for j in range(D // 128):
        cols = slice(j * 128, (j + 1) * 128)
        mixed = (r[:, cols] * scale * gains[j : j + 1]).astype(BF16)
        rows[0, y, x, :, cols] = mixed[:PART]
        rows[1, x, y, :, cols] = mixed[PART:]

    inner, outer = ("x", "y"), ("y", "x")
    inner_at, outer_at = (x, y), (y, x)
    hops = (1, 3, 2)

    def piece(s, o, i):
        return rows.at[s, o % SIDE, i % SIDE]

    def push(s, i, axis):
        b = piece(s, outer_at[s], i)
        return {d: go([remote(b, b, along[axis](d))])[0] for d in hops}

    def each_chip(body):
        def step(d, carry):
            body(lax.rem(req + d, SIDE * SIDE * SIDE))
            return carry

        lax.fori_loop(1, SIDE**3, step, 0)

    def all_but_one(buf, n, k):
        return pltpu.make_async_remote_copy(
            src_ref=buf.at[pl.ds(0, n)], dst_ref=buf.at[pl.ds(0, n)],
            send_sem=gsem.at[k], recv_sem=gsem.at[k + 1], device_id=sibling, device_id_type=MESH,
        )

    def to_chip(src, dst, q, k):
        pltpu.make_async_remote_copy(
            src_ref=src, dst_ref=dst, send_sem=gsem.at[k], recv_sem=gsem.at[k + 1],
            device_id=(q, core), device_id_type=MESH,
        ).start()

    pl.semaphore_wait(all_sem, 3)
    chips = SIDE**3

    @pl.when(core == 1)
    def _():
        tile = jnp.concatenate(
            [resid[HALF - 1 : HALF, j * 128 : (j + 1) * 128] for j in range(16)], axis=0
        )
        last_res[...] = tile
        power = jnp.sum(jnp.sum(tile * tile, axis=1, keepdims=True), axis=0, keepdims=True)
        last_a[req] = (tile * lax.rsqrt(power / D + EPS) * gains[...]).astype(BF16)
        each_chip(lambda q: to_chip(last_a.at[req], last_a.at[req], q, 0))

    one = [push(s, inner_at[s], inner[s]) for s in range(2)]
    two = [{0: push(s, inner_at[s], outer[s])} for s in range(2)]
    got(w_first)
    w_on = go([
        remote(half_shard(zm, core, 0), half_shard(zm, core, 0), along["z"](1)),
        remote(half_shard(zp, core, 1), half_shard(zp, core, 1), along["z"](-1)),
    ])

    def unpack(tiles):
        spread[...] = tiles[...].astype(F32).reshape(chips * 16, 128)
        for j in range(16):
            last_x[:, j * 128 : (j + 1) * 128] = spread[pl.ds(j, chips, stride=16)].astype(BF16)

    got(w_sib[:1])

    @pl.when(core == 1)
    def _():
        all_but_one(last_a, chips - 1, 0).wait_recv()
        unpack(last_a)
        units = pl.ds(unit_at, UNITS)
        lo, hi = last_x[:, : D // 2], last_x[:, D // 2 :]
        gate = nt_dot(lo, wf[0, 0, units]) + nt_dot(hi, wf[1, 0, units])
        up = nt_dot(lo, wf[0, 1, units]) + nt_dot(hi, wf[1, 1, units])
        active = (gate / (1.0 + jnp.exp(-gate)) * up).astype(BF16)
        for h in range(2):
            down = nn_dot(active, wf[h, 2, units])
            for j in range(8):
                spread[pl.ds(8 * h + j, chips, stride=16)] = down[:, j * 128 : (j + 1) * 128]
        last_p[...] = spread[...].reshape(chips, 16, 128).astype(BF16)
        last_in[req] = last_p[req]
        each_chip(lambda q: to_chip(last_p.at[q], last_in.at[req], q, 2))

    for d in (1, 3, 2):
        for s in range(2):
            one[s][d].wait_recv()
            two[s][d] = push(s, inner_at[s] - d + SIDE, outer[s])

    got(w_second)
    w_sib += go([remote(shard(zm, core), shard(zm, core), sibling)])
    w_sib += go([remote(shard(zp, core), shard(zp, core), sibling)])
    got(w_on)
    w_sib += go([remote(shard(zo, core), shard(zo, core), sibling)])

    last_c = remote(last_b.at[req], last_b.at[req], sibling)

    def tell_final():
        def both(q):
            for c in (core, other):
                pltpu.make_async_remote_copy(
                    src_ref=last_b.at[req], dst_ref=last_b.at[req], send_sem=gsem.at[4],
                    recv_sem=gsem.at[5], device_id=(q, c), device_id_type=MESH,
                ).start()

        each_chip(both)

    @pl.when(core == 1)
    def _():
        all_but_one(last_in, chips - 1, 2).wait_recv()
        tile = last_res[...] + jnp.sum(last_in[...].astype(F32), axis=0)
        power = jnp.sum(jnp.sum(tile * tile, axis=1, keepdims=True), axis=0, keepdims=True)
        last_b[req] = (tile * lax.rsqrt(power / D + EPS) * final_gain[...]).astype(BF16)
        last_c.start()
        tell_final()
        last_c.wait_send()

    got(w_sib[1:])
    block_rows = SIDE * PART

    def feed(*ks):
        blocks = [(s, (outer_at[s] + k) % SIDE) for k in ks for s in range(2)]
        xa = jnp.concatenate([rows[s, o].reshape(block_rows, D) for s, o in blocks], axis=0)
        gu = nt_dot(xa[:, : D // 2], wf[0, 0:2].reshape(2 * PLANE_UNITS, D // 2))
        gu += nt_dot(xa[:, D // 2 :], wf[1, 0:2].reshape(2 * PLANE_UNITS, D // 2))
        gate, up = gu[:, :PLANE_UNITS], gu[:, PLANE_UNITS:]
        active = (gate / (1.0 + jnp.exp(-gate)) * up).astype(BF16)
        for j in range(4):
            down = nn_dot(active, wf[j // 2, 2, :, (j % 2) * 512 : (j % 2 + 1) * 512])
            down = down.astype(BF16).reshape(len(blocks), SIDE, PART, 512)
            for b, (s, o) in enumerate(blocks):
                part[s, o, :, :, j * 512 : (j + 1) * 512] = down[b]

    back = [{}, {}]
    near = (2, 1, 3, 0)

    def give_back(k):
        for i in near:
            for s in range(2):
                ii = (inner_at[s] + i) % SIDE
                back[s][k, i] = go([
                    remote(
                        part.at[s, (outer_at[s] + k) % SIDE, ii], in1.at[s, k - 1, i],
                        along[outer[s]](k),
                    )
                ])[0]

    def arrived(d):
        got([two[s][k][d] for k in (0, 1, 3, 2) for s in range(2)])

    arrived(1)
    arrived(3)
    feed(3, 1)
    give_back(3)
    give_back(1)
    arrived(2)
    feed(2)
    give_back(2)
    feed(0)

    @pl.when(core == 0)
    def _():
        last_c.wait_recv()

    all_but_one(last_b, chips - 1, 4).wait_recv()
    unpack(last_b)
    done_with(load_voc)
    pick = (
        order[...] == lax.broadcasted_iota(jnp.int32, (ROWS, ROWS), 0)
    ).astype(BF16)
    final_rows = nn_dot(pick, last_x[...]).astype(BF16)
    top = None
    for start in range(0, VOC, VOC_BLOCK):
        stop = min(start + VOC_BLOCK, VOC)
        block = nt_dot(final_rows, voc[start:stop])
        logp[:, start:stop] = block
        m = jnp.max(block, axis=1, keepdims=True)
        top = m if top is None else jnp.maximum(top, m)
    total = jnp.sum(jnp.exp(logp[...] - top), axis=1, keepdims=True)
    eye = lax.broadcasted_iota(jnp.int32, (ROWS, ROWS), 0) == lax.broadcasted_iota(
        jnp.int32, (ROWS, ROWS), 1
    )

    def as_row(col):
        return jnp.sum(jnp.where(eye, col, 0.0), axis=0, keepdims=True)

    me = req * 2 + core
    stats[me] = jnp.concatenate([as_row(top), as_row(total)], axis=1)

    def tell(d, carry):
        q = lax.rem(me + d, 2 * chips)
        pltpu.make_async_remote_copy(
            src_ref=stats.at[me], dst_ref=stats.at[me], send_sem=gsem.at[6], recv_sem=gsem.at[7],
            device_id=(q // 2, q % 2), device_id_type=MESH,
        ).start()
        return carry

    lax.fori_loop(1, 2 * chips, tell, 0)

    ends = [{}, {}]
    keep = [None, None]
    for k in near:
        for s in range(2):
            got([back[s][o, k] for o in (3, 1, 2)])
            i = (inner_at[s] + k) % SIDE
            tot = part[s, outer_at[s], i].astype(F32)
            for d in range(3):
                tot += in1[s, d, k].astype(F32)
            if k == 0:
                keep[s] = tot
            else:
                mid[s, k - 1] = tot.astype(BF16)
                ends[s][k] = go([remote(mid.at[s, k - 1], in2.at[s, k - 1], along[inner[s]](k))])[0]
    for s in range(2):
        span = slice(s * PART, (s + 1) * PART)
        resid[span] = resid[span] + keep[s]

    all_but_one(stats, 2 * chips - 1, 6).wait_recv()
    tops = stats[:, 0, :ROWS]
    m = jnp.max(tops, axis=0, keepdims=True)
    t = jnp.sum(stats[:, 0, ROWS:] * jnp.exp(tops - m), axis=0, keepdims=True)
    top = jnp.sum(jnp.where(eye, m, 0.0), axis=1, keepdims=True)
    log_total = jnp.sum(jnp.where(eye, jnp.log(t), 0.0), axis=1, keepdims=True)
    logp[...] = logp[...] - top - log_total
    save_logp = local(logp, logp_hbm)
    save_logp.start()

    for s in range(2):
        got([ends[s][k] for k in (2, 1, 3)])
        span = slice(s * PART, (s + 1) * PART)
        tot = resid[span]
        for d in range(3):
            tot += in2[s, d].astype(F32)
        resid[span] = tot
    stay = pl.ds(pl.multiple_of(core * (D // 2), D // 2), D // 2)
    give = pl.ds(pl.multiple_of(other * (D // 2), D // 2), D // 2)
    out_s[...] = resid[:, give].astype(BF16)
    out_x = go([remote(out_s, out_r, sibling)])
    out[mine] = resid[:, stay].astype(BF16)

    @pl.when(core == 1)
    def _():
        all_but_one(last_a, chips - 1, 0).wait_send()
        all_but_one(last_p, chips - 1, 2).wait_send()
        for _ in range(2):
            all_but_one(last_b, chips - 1, 4).wait_send()

    all_but_one(stats, 2 * chips - 1, 6).wait_send()
    for c in sent[:-1]:
        c.wait_send()
    got(out_x)
    out[theirs] = out_r[...]
    save_out = local(out, out_hbm)
    save_out.start()
    out_x[0].wait_send()
    save_logp.wait()
    save_out.wait()


def copy_kernel(a, b, a_out, b_out):
    a_out[...] = a[...]
    b_out[...] = b[...]


def on_device(
    hidden_in, attn_gain, w_query, w_key, w_value, query_gain, key_gain, w_out,
    cache_keys, cache_values, cache_lengths, slot_request, mlp_gain, w_gate, w_up, w_down,
    final_gain, w_vocab,
):
    half_dim = HEAD_DIM // 2
    one = ROPE_BASE ** (-2.0 * np.arange(half_dim) / HEAD_DIM)
    freq = jnp.asarray(np.concatenate([one, one])[None].astype(np.float32))
    vmem = pl.BlockSpec(memory_space=pltpu.VMEM)
    smem = pl.BlockSpec(memory_space=pltpu.SMEM)
    far = pl.BlockSpec(memory_space=pl.ANY)
    V = pltpu.VMEM
    S = SIDE
    results = (
        jax.ShapeDtypeStruct((ROWS, D // 2), BF16),
        jax.ShapeDtypeStruct((ROWS, VOC), F32),
    )
    out, logp = pl.pallas_call(
        step_kernel,
        out_shape=results,
        in_specs=[vmem] * 8 + [smem] * 2 + [far] * 10,
        out_specs=(far, far),
        scratch_shapes=[
            V((ROWS, D // 2), BF16), V((ROWS, VOC), F32),
            V((ROWS, D), BF16),
            V((D, 1024), BF16), V((D, 512), BF16), V((D, 512), BF16), V((1024, D), BF16),
            V((KEYS, 512), BF16), V((KEYS, 512), BF16), V((VOC, D), BF16),
            V((2, 3, PLANE_UNITS, D // 2), BF16),
            V((4, 2 * ROWS, HEAD_DIM), BF16), V((4, ROWS, HEAD_DIM), BF16), V((ROWS, 512), BF16),
            V((ROWS, 1024), BF16), V((ROWS, D), F32), V((HALF, D), F32), V((16, 128), F32),
            V((HALF, D), F32),
            V((2, S, S, PART, D), BF16), V((2, S, S, PART, D), BF16),
            V((2, 3, S, PART, D), BF16), V((2, 3, PART, D), BF16), V((2, 3, PART, D), BF16),
            V((HALF, D // 2), BF16), V((HALF, D // 2), BF16),
            V((S**3, 16, 128), BF16), V((S**3, 16, 128), BF16), V((S**3, 16, 128), BF16),
            V((S**3, 16, 128), BF16), V((16, 128), F32), V((S**3 * 16, 128), F32),
            V((S**3, D), BF16), V((2 * S**3, 1, 128), F32),
            pltpu.SemaphoreType.DMA((32,)),
            pltpu.SemaphoreType.DMA((N_COPIES,)),
            pltpu.SemaphoreType.DMA((N_COPIES,)),
            pltpu.SemaphoreType.DMA((8,)),
            pltpu.SemaphoreType.REGULAR,
            pltpu.SemaphoreType.REGULAR,
        ],
        compiler_params=pltpu.CompilerParams(
            collective_id=0, has_side_effects=True, vmem_limit_bytes=58 * 1024 * 1024
        ),
    )(
        hidden_in, attn_gain.reshape(1, D), query_gain.reshape(1, HEAD_DIM),
        key_gain.reshape(1, HEAD_DIM), mlp_gain.reshape(8, 128), final_gain.reshape(16, 128), freq,
        slot_request.reshape(1, ROWS), slot_request, cache_lengths,
        w_query, w_key, w_value, w_out, cache_keys, cache_values,
        w_gate.T, w_up.T, w_down, w_vocab.T,
    )
    return pl.pallas_call(
        copy_kernel,
        out_shape=results,
        in_specs=[vmem] * 2,
        out_specs=(vmem, vmem),
    )(out, logp)


def solution(mesh):
    in_specs = (
        P("req", None), P(), P(None, "head"), P(None, "head"), P(None, "head"), P(), P(),
        P("head", None), P("req", None, "head"), P("req", None, "head"), P(), P(), P("head"),
        P("head", "req"), P("head", "req"), P("req", "head"), P(), P(None, ("req", "head")),
    )
    out_specs = (P("req", "head"), P(None, ("req", "head")))
    return jax.shard_map(
        on_device, mesh=mesh, in_specs=in_specs, out_specs=out_specs, check_vma=False
    )
```
